256 devices in a mesh: section: 8 (over z), dp: 32 (over x, y, core).
Axes of the slice: x: 4, y: 4, z: 8, core: 2. Of those that a mesh axis runs over, the one named last changes fastest.
Arguments:
- stream: float32 [2, 256, 16, 16, 128], P(None, 'dp'), may hold values from -6 to 6
- cotangent: float32 [2, 256, 16, 16, 128], P(None, 'dp'), may hold values from -6 to 6
- weights: bfloat16 [8, 2304, 128], P('section'), may hold values from -0.09375 to 0.09375
- master: float32 [8, 2304, 128], P('section', 'dp'), may hold values from -0.09375 to 0.09375
- momentum: float32 [8, 2304, 128], P('section', 'dp'), may hold values from -6 to 6
Outputs:
- new_master: float32 [8, 2304, 128], P('section', 'dp')
- new_momentum: float32 [8, 2304, 128], P('section', 'dp')
- new_weights: bfloat16 [8, 2304, 128], P('section')
The draws below stay inside these ranges and needn't reach their ends.
All inputs are finite; a program needn't handle non-finite values.
Results may differ from the reference program's by a relative error of at most 0.014.
Values may be sent and summed in bfloat16 or wider, within the bound.
No kernel may reach another device: no remote copies, remote signals or barrier semaphores. Data moves between devices by JAX's collectives and lax.ppermute only.
A program may use at most 64 MiB of HBM per device.

```python
import jax
import jax.numpy as jnp
from jax import lax

C = 128
SIDE = 16
LAYERS = 1
SECTIONS = 8
IMAGES = 256
ROWS = 2304
N_SECTION = 8


def block_levels(own_key, shape, cuts, least, largest):
    loudness, own = 1.0, jax.random.fold_in(own_key, 6)
    for dim, parts in cuts:
        heights = jnp.exp(jax.random.uniform(jax.random.fold_in(own, dim), (parts,), jnp.float32, least / len(cuts), largest / len(cuts)))
        loudness = loudness * jnp.repeat(heights, shape[dim] // parts).reshape([-1 if axis == dim else 1 for axis in range(len(shape))])
    return loudness


def scatter_about(key, extent, scale, most, split=(), held_as=jnp.bfloat16):
    level = block_levels(key, extent, split, -0.22, 0.18) if split else 1.0
    entries = jax.random.normal(key, extent, jnp.float32) * scale * level
    return jnp.minimum(jnp.maximum(entries, -most), most).astype(held_as)


def setup_inputs(seed: int = 0) -> dict:
    seeds = jax.random.split(jax.random.key(seed), 6)
    stream = scatter_about(seeds[0], (2, IMAGES, SIDE, SIDE, C), 1.0, 6.0, ((1, 32),), jnp.float32)
    cotangent = scatter_about(seeds[1], (2, IMAGES, SIDE, SIDE, C), 1.0, 6.0, ((1, 32),), jnp.float32)
    weights = scatter_about(seeds[2], (SECTIONS, ROWS, C), (36 * C) ** -0.5, 0.09375, ((0, 8),))
    master = scatter_about(seeds[3], (SECTIONS, ROWS, C), (36 * C) ** -0.5, 0.09375, ((0, 8), (1, 32)), jnp.float32)
    momentum = scatter_about(seeds[4], (SECTIONS, ROWS, C), 1.0, 6.0, ((0, 8), (1, 32)), jnp.float32)
    return dict(stream=stream, cotangent=cotangent, weights=weights, master=master, momentum=momentum)


step_size = 0.1
inertia = 0.9

def product(left_op, right_op, dims):
    return lax.dot_general(left_op.astype(jnp.float32), right_op.astype(jnp.float32), (dims, ((), ())), precision=lax.Precision.HIGHEST, preferred_element_type=jnp.float32)

def columns(field):
    height = field.shape[1]
    breadth = field.shape[2]
    padded = jnp.pad(jax.nn.silu(field).astype(jnp.bfloat16), ((0, 0), (1, 1), (1, 1), (0, 0)))
    shifted = [padded[:, row_tap:row_tap + height, col_tap:col_tap + breadth, :] for row_tap in range(3) for col_tap in range(3)]
    return jnp.concatenate(shifted, axis=3).reshape(-1, 9 * field.shape[3])

def convolve(patches, weight, template):
    return product(patches, weight, ((1,), (0,))).reshape(template.shape)

def spread(rounded, weight, template):
    height, breadth, channels = (template.shape[1], template.shape[2], template.shape[3])
    spread_cols = product(rounded, weight, ((1,), (1,))).reshape(template.shape[0], height, breadth, 9 * channels)
    padded = jnp.pad(spread_cols, ((0, 0), (1, 1), (1, 1), (0, 0)))
    summed = jnp.zeros(template.shape, jnp.float32)
    for row_tap in range(3):
        for col_tap in range(3):
            tap_index = 3 * row_tap + col_tap
            summed = summed + padded[:, 2 - row_tap:2 - row_tap + height, 2 - col_tap:2 - col_tap + breadth, tap_index * channels:(tap_index + 1) * channels]
    return summed

def weight_grad(patches, rounded):
    return product(patches, rounded, ((0,), (0,)))

def silu_slope(field):
    logistic = jax.nn.sigmoid(field)
    return logistic * (1.0 + field * (1.0 - logistic))

def coupling_forward(first, second, weight_f, weight_g):
    patch_f = columns(second)
    out_first = first + convolve(patch_f, weight_f, second)
    patch_g = columns(out_first)
    out_second = second + convolve(patch_g, weight_g, out_first)
    return (out_first, out_second)

def coupling_backward(out_first, out_second, grad_first, grad_second, weight_f, weight_g):
    channels = out_first.shape[3]
    patch_g = columns(out_first)
    second = out_second - convolve(patch_g, weight_g, out_first)
    patch_f = columns(second)
    first = out_first - convolve(patch_f, weight_f, second)
    round_second = grad_second.astype(jnp.bfloat16).reshape(-1, channels)
    wgrad_g = weight_grad(patch_g, round_second)
    grad_first = grad_first + spread(round_second, weight_g, out_first) * silu_slope(out_first)
    round_first = grad_first.astype(jnp.bfloat16).reshape(-1, channels)
    wgrad_f = weight_grad(patch_f, round_first)
    grad_second = grad_second + spread(round_first, weight_f, second) * silu_slope(second)
    return (first, second, grad_first, grad_second, wgrad_f, wgrad_g)

def reference(stream, cotangent, weights, master, momentum):
    blocks = weights.reshape(N_SECTION, LAYERS, 2, 9 * C, C)
    first, second = (stream[0], stream[1])
    for section_idx in range(N_SECTION):
        for coupling in range(LAYERS):
            first, second = coupling_forward(first, second, blocks[section_idx, coupling, 0], blocks[section_idx, coupling, 1])
    grad_first, grad_second = (cotangent[0], cotangent[1])
    section_grads = []
    for section_idx in reversed(range(N_SECTION)):
        pieces = []
        for coupling in reversed(range(LAYERS)):
            first, second, grad_first, grad_second, wgrad_f, wgrad_g = coupling_backward(first, second, grad_first, grad_second, blocks[section_idx, coupling, 0], blocks[section_idx, coupling, 1])
            pieces.append(jnp.stack([wgrad_f, wgrad_g]))
        pieces = pieces[::-1]
        section_grads.append(jnp.stack(pieces).reshape(LAYERS * 18 * C, C))
    section_grads = section_grads[::-1]
    gradient = jnp.stack(section_grads) / IMAGES
    new_momentum = inertia * momentum + gradient
    new_master = master - step_size * new_momentum
    return (new_master, new_momentum, new_master.astype(jnp.bfloat16))
```

```python
import jax
import jax.numpy as jnp
from jax import lax
from jax.experimental import pallas as pl
from jax.experimental.pallas import tpu as pltpu
from jax.sharding import PartitionSpec as P

STEP_SIZE = 0.1
INERTIA = 0.9
ROUND = jnp.bfloat16


def image_step(sections, side, rows, slot, stream, cotangent, weights, grads, x_in, d_in, w_all, g_all,
               saved_p, slopes, fwd_pad, bwd_pad, x_sem, w_sem, g_sem):
    channels = stream.shape[-1]
    pixels = side * side
    half = rows // 2
    x_copy = pltpu.make_async_copy(stream.at[:, slot[0]], x_in, x_sem.at[0])
    d_copy = pltpu.make_async_copy(cotangent.at[:, slot[0]], d_in, x_sem.at[1])
    x_copy.start()

    def w_copy(s):
        part = pl.ds(s * rows, rows)
        return pltpu.make_async_copy(weights.at[part, :], w_all.at[part, :], w_sem.at[s])

    def g_copy(s):
        part = pl.ds(s * rows, rows)
        return pltpu.make_async_copy(g_all.at[part, :], grads.at[part, :], g_sem.at[s])

    for s in range(sections):
        w_copy(s).start()
    d_copy.start()
    edge = jnp.zeros((side, 3 * channels), ROUND)
    for pad in (fwd_pad, bwd_pad):
        for k in range(2):
            pad[k, 0:side, :] = edge
            pad[k, side + pixels : 2 * side + pixels, :] = edge

    column = lax.broadcasted_iota(jnp.int32, (pixels, channels), 0) & (side - 1)
    not_first = column > 0
    not_last = column < side - 1

    def before(v):
        return jnp.where(not_first, pltpu.roll(v, 1, 0), 0.0).astype(ROUND)

    def after(v):
        return jnp.where(not_last, pltpu.roll(v, pixels - 1, 0), 0.0).astype(ROUND)

    def band(pad, k, low, mid, high):
        body = pl.ds(side, pixels)
        pad[k, body, 0:channels] = low
        pad[k, body, channels : 2 * channels] = mid
        pad[k, body, 2 * channels : 3 * channels] = high

    def conv(pad, k, w):
        taps = jnp.concatenate([pad[k, a * side : a * side + pixels, :] for a in range(3)], axis=1)
        return jnp.dot(taps, w, preferred_element_type=jnp.float32)

    def activate(v, at):
        logistic = 1.0 / (1.0 + jnp.exp(-v))
        p = v * logistic
        slopes[at] = logistic + p * (1.0 - logistic)
        saved_p[at] = p.T.astype(ROUND)
        return p

    def forward(s, pair):
        x1, x2 = pair
        w_copy(s).wait()
        base = pl.multiple_of(s * rows, rows)
        p = activate(x2, 2 * s)
        band(fwd_pad, 0, before(p), p.astype(ROUND), after(p))
        y1 = x1 + conv(fwd_pad, 0, w_all[pl.ds(base, half), :])
        p = activate(y1, 2 * s + 1)
        band(fwd_pad, 1, before(p), p.astype(ROUND), after(p))
        y2 = x2 + conv(fwd_pad, 1, w_all[pl.ds(base + half, half), :])
        return y1, y2

    x_copy.wait()
    lax.fori_loop(0, sections, forward, (x_in[0], x_in[1]))

    def spread(k, e, base, at):
        band(bwd_pad, k, after(e), e.astype(ROUND), before(e))
        total = None
        pieces = []
        for a in range(3):
            lines = bwd_pad[k, (2 - a) * side : (2 - a) * side + pixels, :]
            pieces.append(lines)
            for b in range(3):
                w = w_all[pl.ds(base + (3 * a + b) * channels, channels), :]
                part = lax.dot_general(
                    lines[:, b * channels : (b + 1) * channels], w, (((1,), (1,)), ((), ())),
                    preferred_element_type=jnp.float32,
                )
                total = part if total is None else total + part
        wgrad = jnp.dot(
            saved_p[at], jnp.concatenate(pieces, axis=1), preferred_element_type=jnp.float32
        ).astype(ROUND)
        for tap in range(9):
            g_all[pl.ds(base + tap * channels, channels), :] = wgrad[:, tap * channels : (tap + 1) * channels]
        return total * slopes[at]

    def backward(step, pair):
        d1, d2 = pair
        s = sections - 1 - step
        base = pl.multiple_of(s * rows, rows)
        d1 = d1 + spread(0, d2, base + half, 2 * s + 1)
        d2 = d2 + spread(1, d1, base, 2 * s)
        g_copy(s).start()
        return d1, d2

    d_copy.wait()
    lax.fori_loop(0, sections, backward, (d_in[0], d_in[1]))
    for s in range(sections):
        g_copy(s).wait()


def image_grads(stream, cotangent, weights, which, sections):
    side, channels = stream.shape[2], stream.shape[4]
    pixels = side * side
    images = stream.shape[1]
    rows = weights.shape[0] // sections
    flat = (2, images, pixels, channels)
    far = pl.BlockSpec(memory_space=pltpu.HBM)
    kernel = lambda *refs: image_step(sections, side, rows, *refs)
    return pl.pallas_call(
        kernel,
        out_shape=jax.ShapeDtypeStruct(weights.shape, ROUND),
        grid_spec=pltpu.PrefetchScalarGridSpec(
            num_scalar_prefetch=1,
            grid=(1,),
            in_specs=[far, far, far],
            out_specs=far,
            scratch_shapes=[
                pltpu.VMEM((2, pixels, channels), jnp.float32),
                pltpu.VMEM((2, pixels, channels), jnp.float32),
                pltpu.VMEM(weights.shape, ROUND),
                pltpu.VMEM(weights.shape, ROUND),
                pltpu.VMEM((2 * sections, channels, pixels), ROUND),
                pltpu.VMEM((2 * sections, pixels, channels), jnp.float32),
                pltpu.VMEM((2, pixels + 2 * side, 3 * channels), ROUND),
                pltpu.VMEM((2, pixels + 2 * side, 3 * channels), ROUND),
                pltpu.SemaphoreType.DMA((2,)),
                pltpu.SemaphoreType.DMA((sections,)),
                pltpu.SemaphoreType.DMA((sections,)),
            ],
        ),
        compiler_params=pltpu.CompilerParams(vmem_limit_bytes=60 << 20),
        name="image_step",
    )(which, stream.reshape(flat), cotangent.reshape(flat), weights)


def on_device(stream, cotangent, weights, master, momentum):
    sections = lax.axis_size("section")
    dp = lax.axis_size("dp")
    images = stream.shape[1] * dp
    share = weights.shape[1] // dp
    channels = weights.shape[2]
    every = lax.all_gather(weights[0], "section", axis=0, tiled=True)
    which = lax.axis_index("section").astype(jnp.int32).reshape(1)
    grads = image_grads(stream, cotangent, every, which, sections)
    own = lax.psum_scatter(grads, "section", scatter_dimension=0, tiled=True)
    tiles = lax.all_to_all(own.reshape(dp, share, channels), "dp", 0, 0, tiled=True)
    gradient = jnp.sum(tiles.astype(jnp.float32), axis=0) / images
    new_momentum = INERTIA * momentum[0] + gradient
    new_master = master[0] - STEP_SIZE * new_momentum
    copies = jnp.broadcast_to(new_master.astype(ROUND)[None], (dp, share, channels))
    new_weights = lax.all_to_all(copies, "dp", 0, 0, tiled=True).reshape(dp * share, channels)
    return (new_master[None], new_momentum[None], new_weights[None])


def solution(mesh):
    placed = (
        P(None, "dp", None, None, None),
        P(None, "dp", None, None, None),
        P("section", None, None),
        P("section", "dp", None),
        P("section", "dp", None),
    )
    return jax.shard_map(
        on_device,
        mesh=mesh,
        in_specs=placed,
        out_specs=(P("section", "dp", None), P("section", "dp", None), P("section", None, None)),
        check_vma=False,
    )
```

```python
import jax
import jax.numpy as jnp
from jax import lax
from jax.experimental import pallas as pl
from jax.experimental.pallas import tpu as pltpu
from jax.sharding import PartitionSpec as P

STEP_SIZE = 0.1
INERTIA = 0.9
ROUND = jnp.bfloat16


def chip(role, first, second):
    return jnp.where(role == 0, second, first), jnp.where(role == 0, first, second)


def image_step(sides, sections, side, share, place, stream, cotangent, *refs):
    gathered, refs = refs[:10], refs[10:]
    kept, passed, refs = refs[0], refs[1:5], refs[5:]
    x_in, d_in, w_all, g_all, saved_p, slopes, fwd_pad, bwd_pad, x_sem, w_sem, g_sem = refs
    z, x, y, core = place[0], place[1], place[2], place[3]
    channels = stream.shape[-1]
    pixels = side * side
    rows = w_all.shape[1]
    half = rows // 2
    x_copy = pltpu.make_async_copy(stream.at[:, z], x_in, x_sem.at[0])
    d_copy = pltpu.make_async_copy(cotangent.at[:, z], d_in, x_sem.at[1])

    def block(role, at_first, at_second):
        first = jnp.where(role == 0, y, x)
        second = jnp.where(role == 0, x, y)
        px, py = chip(role, lax.rem(first + at_first + sides, sides), lax.rem(second + at_second + sides, sides))
        return pl.ds(pl.multiple_of(((px * sides + py) * 2 + role) * share, 8), share)

    copies = []
    for which in range(2):
        role = core if which == 0 else 1 - core
        near, low, high, far_a, far_b = gathered[5 * which : 5 * which + 5]
        for i in range(sides):
            far = far_a.at[i] if i < sides // 2 else far_b.at[i - sides // 2]
            for j, source in enumerate((near.at[i], low.at[i], far, high.at[i])):
                target = w_all.at[:, block(role, -i, -j), :]
                copies.append(pltpu.make_async_copy(source, target, w_sem.at[len(copies)]))
    x_copy.start()
    for copy in copies:
        copy.start()
    d_copy.start()
    edge = jnp.zeros((side, 3 * channels), ROUND)
    for pad in (fwd_pad, bwd_pad):
        for k in range(2):
            pad[k, 0:side, :] = edge
            pad[k, side + pixels : 2 * side + pixels, :] = edge

    column = lax.broadcasted_iota(jnp.int32, (pixels, channels), 0) & (side - 1)
    not_first = column > 0
    not_last = column < side - 1

    def before(v):
        return jnp.where(not_first, pltpu.roll(v, 1, 0), 0.0).astype(ROUND)

    def after(v):
        return jnp.where(not_last, pltpu.roll(v, pixels - 1, 0), 0.0).astype(ROUND)

    def band(pad, k, low, mid, high):
        body = pl.ds(side, pixels)
        pad[k, body, 0:channels] = low
        pad[k, body, channels : 2 * channels] = mid
        pad[k, body, 2 * channels : 3 * channels] = high

    def conv(pad, k, w):
        taps = jnp.concatenate([pad[k, a * side : a * side + pixels, :] for a in range(3)], axis=1)
        return jnp.dot(taps, w, preferred_element_type=jnp.float32)

    def activate(v, at):
        logistic = 1.0 / (1.0 + jnp.exp(-v))
        p = v * logistic
        slopes[at] = logistic + p * (1.0 - logistic)
        saved_p[at] = p.T.astype(ROUND)
        return p

    def forward(s, pair):
        x1, x2 = pair
        w = w_all.at[lax.rem(z - s + sections, sections)]
        p = activate(x2, 2 * s)
        band(fwd_pad, 0, before(p), p.astype(ROUND), after(p))
        y1 = x1 + conv(fwd_pad, 0, w[0:half, :])
        p = activate(y1, 2 * s + 1)
        band(fwd_pad, 1, before(p), p.astype(ROUND), after(p))
        y2 = x2 + conv(fwd_pad, 1, w[half:rows, :])
        return y1, y2

    x_copy.wait()
    for copy in copies:
        copy.wait()
    lax.fori_loop(0, sections, forward, (x_in[0], x_in[1]))

    def spread(k, e, w, g, base, at):
        band(bwd_pad, k, after(e), e.astype(ROUND), before(e))
        total = None
        pieces = []
        for a in range(3):
            lines = bwd_pad[k, (2 - a) * side : (2 - a) * side + pixels, :]
            pieces.append(lines)
            for b in range(3):
                first = base + (3 * a + b) * channels
                part = lax.dot_general(
                    lines[:, b * channels : (b + 1) * channels], w[first : first + channels, :],
                    (((1,), (1,)), ((), ())), preferred_element_type=jnp.float32,
                )
                total = part if total is None else total + part
        wgrad = jnp.dot(
            saved_p[at], jnp.concatenate(pieces, axis=1), preferred_element_type=jnp.float32
        ).astype(ROUND)
        for tap in range(9):
            first = base + tap * channels
            g[first : first + channels, :] = wgrad[:, tap * channels : (tap + 1) * channels]
        return total * slopes[at]

    def backward(step, pair):
        d1, d2 = pair
        s = sections - 1 - step
        w = w_all.at[lax.rem(z - s + sections, sections)]
        g = g_all.at[lax.rem(s - z + sections, sections)]
        d1 = d1 + spread(0, d2, w, g, half, 2 * s + 1)
        d2 = d2 + spread(1, d1, w, g, 0, 2 * s)
        return d1, d2

    d_copy.wait()
    lax.fori_loop(0, sections, backward, (d_in[0], d_in[1]))
    copies = []
    for j in (2, 1, 3, 0):
        for i in range(sides):
            for role, target in ((1 - core, passed[j].at[i]), (core, kept.at[j, i])):
                source = g_all.at[:, block(role, i, j), :]
                copies.append(pltpu.make_async_copy(source, target, g_sem.at[len(copies)]))
    for copy in copies:
        copy.start()
    for copy in copies:
        copy.wait()


def image_grads(stream, cotangent, gathered, place, sides):
    side, channels = stream.shape[2], stream.shape[4]
    pixels = side * side
    images = stream.shape[1]
    sections, share = gathered[0].shape[1:3]
    rows = share * 2 * sides * sides
    flat = (2, images, pixels, channels)
    far = pl.BlockSpec(memory_space=pltpu.HBM)
    kernel = lambda *refs: image_step(sides, sections, side, share, *refs)
    piece = (sides, sections, share, channels)
    return pl.pallas_call(
        kernel,
        out_shape=[jax.ShapeDtypeStruct((sides, *piece), ROUND)] + [jax.ShapeDtypeStruct(piece, ROUND)] * sides,
        grid_spec=pltpu.PrefetchScalarGridSpec(
            num_scalar_prefetch=1,
            grid=(1,),
            in_specs=[far] * 12,
            out_specs=[far] * 5,
            scratch_shapes=[
                pltpu.VMEM((2, pixels, channels), jnp.float32),
                pltpu.VMEM((2, pixels, channels), jnp.float32),
                pltpu.VMEM((sections, rows, channels), ROUND),
                pltpu.VMEM((sections, rows, channels), ROUND),
                pltpu.VMEM((2 * sections, channels, pixels), ROUND),
                pltpu.VMEM((2 * sections, pixels, channels), jnp.float32),
                pltpu.VMEM((2, pixels + 2 * side, 3 * channels), ROUND),
                pltpu.VMEM((2, pixels + 2 * side, 3 * channels), ROUND),
                pltpu.SemaphoreType.DMA((2,)),
                pltpu.SemaphoreType.DMA((2 * sides * sides,)),
                pltpu.SemaphoreType.DMA((2 * sides * sides,)),
            ],
        ),
        compiler_params=pltpu.CompilerParams(vmem_limit_bytes=60 << 20),
        name="image_step",
    )(place, stream.reshape(flat), cotangent.reshape(flat), *gathered)


def along_z(value, by):
    n = lax.axis_size("section")
    return lax.ppermute(value, "section", [(i, (i + by) % n) for i in range(n)])


def in_plane(sides, value, to):
    pairs = []
    for x in range(sides):
        for y in range(sides):
            for core in range(2):
                px, py, pc = to(x, y, core)
                pairs.append(((x * sides + y) * 2 + core, ((px % sides) * sides + py % sides) * 2 + pc))
    return lax.ppermute(value, "dp", pairs)


def along_first(sides, value, by):
    return in_plane(sides, value, lambda x, y, c: (x, y + by, c) if c == 0 else (x + by, y, c))


def along_second(sides, value, by):
    return in_plane(sides, value, lambda x, y, c: (x + by, y, c) if c == 0 else (x, y + by, c))


def swapped(sides, value):
    return in_plane(sides, value, lambda x, y, c: (x, y, 1 - c))


def gather_weights(mine, sections, sides):
    line = jnp.stack([mine] + [along_z(mine, k) for k in range(1, sections)])
    near = jnp.stack([line] + [along_first(sides, line, i) for i in range(1, sides)])
    middle = sides // 2
    low = along_second(sides, near, 1)
    high = along_second(sides, near, -1)
    far_a = along_second(sides, low[:middle], 1)
    far_b = along_second(sides, high[middle:], -1)
    own = [near, low, high, far_a, far_b]
    return own + [swapped(sides, block) for block in own]


def wide(value):
    return value.astype(jnp.float32)


def scatter_grads(kept, passed, sections, sides):
    middle = sides // 2
    came = {j: swapped(sides, passed[j]) for j in (2, 1, 3, 0)}
    opposite = wide(kept[2]) + wide(came[2])
    opposite = opposite.astype(ROUND)
    a_in = along_second(sides, opposite[:middle], 1)
    b_in = along_second(sides, opposite[middle:], -1)
    one, three = kept[1], kept[3]
    one_b = (wide(one[middle:]) + wide(came[1][middle:])).astype(ROUND)
    three_a = (wide(three[:middle]) + wide(came[3][:middle])).astype(ROUND)
    low_b = along_second(sides, one_b, 1)
    high_a = along_second(sides, three_a, -1)
    one_a = (wide(one[:middle]) + wide(came[1][:middle]) + wide(a_in)).astype(ROUND)
    three_b = (wide(three[middle:]) + wide(came[3][middle:]) + wide(b_in)).astype(ROUND)
    low_a = along_second(sides, one_a, 1)
    high_b = along_second(sides, three_b, -1)
    low = jnp.concatenate([low_a, low_b])
    high = jnp.concatenate([high_a, high_b])
    mine = (wide(kept[0]) + wide(came[0]) + wide(low) + wide(high)).astype(ROUND)
    line = wide(mine[0])
    for i in range(1, sides):
        line = line + wide(along_first(sides, mine[i], i))
    line = line.astype(ROUND)
    total = wide(line[0])
    for k in range(1, sections):
        total = total + wide(along_z(line[k], k))
    return total


def on_device(stream, cotangent, weights, master, momentum):
    sections = lax.axis_size("section")
    dp = lax.axis_size("dp")
    sides = int(round((dp // 2) ** 0.5))
    images = stream.shape[1] * dp
    share = weights.shape[1] // dp
    channels = weights.shape[2]
    z, at = lax.axis_index("section"), lax.axis_index("dp")
    place = jnp.stack([z, at // (2 * sides), at // 2 % sides, at % 2]).astype(jnp.int32)
    mine = lax.dynamic_slice_in_dim(weights[0], at * share, share, 0)
    gathered = gather_weights(mine, sections, sides)
    kept, *passed = image_grads(stream, cotangent, gathered, place, sides)
    gradient = scatter_grads(kept, passed, sections, sides) / images
    new_momentum = INERTIA * momentum[0] + gradient
    new_master = master[0] - STEP_SIZE * new_momentum
    copies = jnp.broadcast_to(new_master.astype(ROUND)[None], (dp, share, channels))
    new_weights = lax.all_to_all(copies, "dp", 0, 0, tiled=True).reshape(dp * share, channels)
    return (new_master[None], new_momentum[None], new_weights[None])


def solution(mesh):
    placed = (
        P(None, "dp", None, None, None),
        P(None, "dp", None, None, None),
        P("section", None, None),
        P("section", "dp", None),
        P("section", "dp", None),
    )
    return jax.shard_map(
        on_device,
        mesh=mesh,
        in_specs=placed,
        out_specs=(P("section", "dp", None), P("section", "dp", None), P("section", None, None)),
        check_vma=False,
    )
```

```python
import jax
import jax.numpy as jnp
from jax import lax
from jax.experimental import pallas as pl
from jax.experimental.pallas import tpu as pltpu
from jax.sharding import PartitionSpec as P

STEP_SIZE = 0.1
INERTIA = 0.9
ROUND = jnp.bfloat16
VMEM = 24


ORDERS = ((0, 1, 3, 2), (0, 3, 1, 2))
FIRST = ORDERS[0]


def reversed_bits(r):
    return ((r & 1) << 2) | (r & 2) | (r >> 2)


def image_step(sides, sections, side, share, place, stream, cotangent, *refs):
    gathered, refs = refs[:10], refs[10:]
    outs, refs = refs[:8], refs[8:]
    x_in, d_in, w_all, g_all, saved_p, slopes, fwd_pad, bwd_pad, x_sem, w_sem, g_sem = refs
    z, x, y, core = place[0], place[1], place[2], place[3]
    channels = stream.shape[-1]
    pixels = side * side
    rows = w_all.shape[1]
    half = rows // 2
    slots = sections // 2
    x_copy = pltpu.make_async_copy(stream, x_in, x_sem.at[0])
    d_copy = pltpu.make_async_copy(cotangent, d_in, x_sem.at[1])

    def block(role, part, i, j):
        first, second = FIRST[i], ORDERS[part][j]
        px = x ^ jnp.where(role == 0, second, first)
        py = y ^ jnp.where(role == 0, first, second)
        start = pl.multiple_of(((px * sides + py) * 2 + role) * share, 8)
        return pl.ds(part * slots, slots), pl.ds(start, share)

    copies = []
    for which in range(2):
        role = core if which == 0 else 1 - core
        near, one_a, one_b, two_a, two_b = gathered[5 * which : 5 * which + 5]
        for part, (one, two) in enumerate(((one_a, two_a), (one_b, two_b))):
            for i in range(sides):
                for j, source in enumerate((near.at[part, i], one.at[i], two.at[0, i], two.at[1, i])):
                    where, lines = block(role, part, i, j)
                    target = w_all.at[where, lines, :]
                    copies.append(pltpu.make_async_copy(source, target, w_sem.at[len(copies)]))
    x_copy.start()
    for copy in copies:
        copy.start()
    d_copy.start()
    edge = jnp.zeros((side, 3 * channels), ROUND)
    for pad in (fwd_pad, bwd_pad):
        for k in range(2):
            pad[k, 0:side, :] = edge
            pad[k, side + pixels : 2 * side + pixels, :] = edge

    column = lax.broadcasted_iota(jnp.int32, (pixels, channels), 0) & (side - 1)
    not_first = column > 0
    not_last = column < side - 1

    def before(v):
        return jnp.where(not_first, pltpu.roll(v, 1, 0), 0.0).astype(ROUND)

    def after(v):
        return jnp.where(not_last, pltpu.roll(v, pixels - 1, 0), 0.0).astype(ROUND)

    def band(pad, k, low, mid, high):
        body = pl.ds(side, pixels)
        pad[k, body, 0:channels] = low
        pad[k, body, channels : 2 * channels] = mid
        pad[k, body, 2 * channels : 3 * channels] = high

    def conv(pad, k, w):
        taps = jnp.concatenate([pad[k, a * side : a * side + pixels, :] for a in range(3)], axis=1)
        return jnp.dot(taps, w, preferred_element_type=jnp.float32)

    def activate(v, at):
        logistic = 1.0 / (1.0 + jnp.exp(-v))
        p = v * logistic
        slopes[at] = logistic + p * (1.0 - logistic)
        saved_p[at] = p.T.astype(ROUND)
        return p

    def forward(s, pair):
        x1, x2 = pair
        w = w_all.at[reversed_bits(z ^ s)]
        p = activate(x2, 2 * s)
        band(fwd_pad, 0, before(p), p.astype(ROUND), after(p))
        y1 = x1 + conv(fwd_pad, 0, w[0:half, :])
        p = activate(y1, 2 * s + 1)
        band(fwd_pad, 1, before(p), p.astype(ROUND), after(p))
        y2 = x2 + conv(fwd_pad, 1, w[half:rows, :])
        return y1, y2

    x_copy.wait()
    for copy in copies:
        copy.wait()
    lax.fori_loop(0, sections, forward, (x_in[0], x_in[1]))

    def spread(k, e, w, g, base, at):
        band(bwd_pad, k, after(e), e.astype(ROUND), before(e))
        total = None
        pieces = []
        for a in range(3):
            lines = bwd_pad[k, (2 - a) * side : (2 - a) * side + pixels, :]
            pieces.append(lines)
            for b in range(3):
                first = base + (3 * a + b) * channels
                part = lax.dot_general(
                    lines[:, b * channels : (b + 1) * channels], w[first : first + channels, :],
                    (((1,), (1,)), ((), ())), preferred_element_type=jnp.float32,
                )
                total = part if total is None else total + part
        wgrad = jnp.dot(
            saved_p[at], jnp.concatenate(pieces, axis=1), preferred_element_type=jnp.float32
        ).astype(ROUND)
        for tap in range(9):
            first = base + tap * channels
            g[first : first + channels, :] = wgrad[:, tap * channels : (tap + 1) * channels]
        return total * slopes[at]

    def backward(step, pair):
        d1, d2 = pair
        s = sections - 1 - step
        w = w_all.at[reversed_bits(z ^ s)]
        g = g_all.at[reversed_bits(z ^ s)]
        d1 = d1 + spread(0, d2, w, g, half, 2 * s + 1)
        d2 = d2 + spread(1, d1, w, g, 0, 2 * s)
        return d1, d2

    d_copy.wait()
    lax.fori_loop(0, sections, backward, (d_in[0], d_in[1]))
    copies = []
    for first_j in (2, 0):
        for part in range(2):
            passed, kept = outs[2 * part + 1 - first_j // 2], outs[4 + 2 * part + 1 - first_j // 2]
            for i in range(sides):
                for j in range(2):
                    for role, target in ((1 - core, passed.at[j, i]), (core, kept.at[j, i])):
                        where, lines = block(role, part, i, first_j + j)
                        source = g_all.at[where, lines, :]
                        copies.append(pltpu.make_async_copy(source, target, g_sem.at[len(copies)]))
    for copy in copies:
        copy.start()
    for copy in copies:
        copy.wait()


def image_grads(stream, cotangent, gathered, place, sides):
    pixels, channels = stream.shape[1:]
    side = int(round(pixels**0.5))
    share = gathered[0].shape[3]
    sections = 2 * gathered[0].shape[2]
    rows = share * 2 * sides * sides
    far = pl.BlockSpec(memory_space=pl.ANY)
    kernel = lambda *refs: image_step(sides, sections, side, share, *refs)
    pair = (2, sides, sections // 2, share, channels)
    return pl.pallas_call(
        kernel,
        out_shape=[jax.ShapeDtypeStruct(pair, ROUND)] * 8,
        grid_spec=pltpu.PrefetchScalarGridSpec(
            num_scalar_prefetch=1,
            grid=(1,),
            in_specs=[far] * 12,
            out_specs=[far] * 8,
            scratch_shapes=[
                pltpu.VMEM((2, pixels, channels), jnp.float32),
                pltpu.VMEM((2, pixels, channels), jnp.float32),
                pltpu.VMEM((sections, rows, channels), ROUND),
                pltpu.VMEM((sections, rows, channels), ROUND),
                pltpu.VMEM((2 * sections, channels, pixels), ROUND),
                pltpu.VMEM((2 * sections, pixels, channels), jnp.float32),
                pltpu.VMEM((2, pixels + 2 * side, 3 * channels), ROUND),
                pltpu.VMEM((2, pixels + 2 * side, 3 * channels), ROUND),
                pltpu.SemaphoreType.DMA((2,)),
                pltpu.SemaphoreType.DMA((4 * sides * sides,)),
                pltpu.SemaphoreType.DMA((4 * sides * sides,)),
            ],
        ),
        compiler_params=pltpu.CompilerParams(vmem_limit_bytes=VMEM << 20),
        name="image_step",
    )(place, stream, cotangent, *gathered)


def along_z(value, mask):
    n = lax.axis_size("section")
    return lax.ppermute(value, "section", [(i, i ^ mask) for i in range(n)])


def in_plane(sides, value, to):
    pairs = []
    for x in range(sides):
        for y in range(sides):
            for core in range(2):
                px, py, pc = to(x, y, core)
                pairs.append(((x * sides + y) * 2 + core, (px * sides + py) * 2 + pc))
    return lax.ppermute(value, "dp", pairs)


def along_first(sides, value, mask):
    return in_plane(sides, value, lambda x, y, c: (x, y ^ mask, c) if c == 0 else (x ^ mask, y, c))


def along_second(sides, value, mask):
    return in_plane(sides, value, lambda x, y, c: (x ^ mask, y, c) if c == 0 else (x, y ^ mask, c))


def swapped(sides, value):
    return in_plane(sides, value, lambda x, y, c: (x, y, 1 - c))


def gather_weights(mine, sides):
    line = mine[None]
    for mask in (4, 2):
        line = jnp.concatenate([line, along_z(line, mask)])
    line = jnp.stack([line, along_z(line, 1)])[:, None]
    for mask in (1, 3):
        line = jnp.concatenate([line, along_first(sides, line, mask)], axis=1)
    zero_a, zero_b = line[0], line[1]
    one_a = along_second(sides, zero_a, 1)
    one_b = along_second(sides, zero_b, 3)
    two_a = along_second(sides, jnp.stack([zero_a, one_a]), 3)
    two_b = along_second(sides, jnp.stack([zero_b, one_b]), 1)
    own = [line, one_a, one_b, two_a, two_b]
    return own + [swapped(sides, block) for block in own]


def wide(value):
    return value.astype(jnp.float32)


def scatter_grads(blocks, sides):
    passed, kept = blocks[:4], blocks[4:]
    late = [None, None]
    for part in range(2):
        late[part] = swapped(sides, passed[2 * part])
    soon = [None, None]
    for part in range(2):
        soon[part] = swapped(sides, passed[2 * part + 1])
    came = []
    for part in range(2):
        out = (wide(kept[2 * part]) + wide(late[part])).astype(ROUND)
        came.append(along_second(sides, out, (3, 1)[part]))
    parts = []
    for part in range(2):
        near = kept[2 * part + 1]
        out = (wide(near[1]) + wide(soon[part][1]) + wide(came[part][1])).astype(ROUND)
        last = along_second(sides, out, (1, 3)[part])
        parts.append(wide(near[0]) + wide(soon[part][0]) + wide(came[part][0]) + wide(last))
    line = jnp.stack(parts).astype(ROUND)
    got = along_first(sides, line[:, 2:], 3)
    line = wide(line[:, :2]) + wide(got)
    got = along_first(sides, line[:, 1].astype(ROUND), 1)
    line = line[:, 0] + wide(got)
    got = along_z(line[1].astype(ROUND), 1)
    line = line[0] + wide(got)
    for mask in (2, 4):
        middle = line.shape[0] // 2
        got = along_z(line[middle:].astype(ROUND), mask)
        line = line[:middle] + wide(got)
    return line[0]


def on_device(stream, cotangent, weights, master, momentum):
    dp = lax.axis_size("dp")
    sides = int(round((dp // 2) ** 0.5))
    images = stream.shape[1] * dp
    share = weights.shape[1] // dp
    channels = weights.shape[2]
    z, at = lax.axis_index("section"), lax.axis_index("dp")
    place = jnp.stack([z, at // (2 * sides), at // 2 % sides, at % 2]).astype(jnp.int32)
    mine = lax.dynamic_slice_in_dim(weights[0], at * share, share, 0)
    gathered = gather_weights(mine, sides)
    pair = (2, stream.shape[2] * stream.shape[3], channels)
    first, last = (lax.dynamic_slice_in_dim(v, z, 1, 1).reshape(pair) for v in (stream, cotangent))
    blocks = image_grads(first, last, gathered, place, sides)
    gradient = scatter_grads(blocks, sides) / images
    new_momentum = INERTIA * momentum[0] + gradient
    new_master = master[0] - STEP_SIZE * new_momentum
    copies = jnp.broadcast_to(new_master.astype(ROUND)[None], (dp, share, channels))
    new_weights = lax.all_to_all(copies, "dp", 0, 0, tiled=True).reshape(dp * share, channels)
    return (new_master[None], new_momentum[None], new_weights[None])


def solution(mesh):
    placed = (
        P(None, "dp", None, None, None),
        P(None, "dp", None, None, None),
        P("section", None, None),
        P("section", "dp", None),
        P("section", "dp", None),
    )
    return jax.shard_map(
        on_device,
        mesh=mesh,
        in_specs=placed,
        out_specs=(P("section", "dp", None), P("section", "dp", None), P("section", None, None)),
        check_vma=False,
    )
```

```python
import jax
import jax.numpy as jnp
from jax import lax
from jax.experimental import pallas as pl
from jax.experimental.pallas import tpu as pltpu
from jax.sharding import PartitionSpec as P

STEP_SIZE = 0.1
INERTIA = 0.9
ROUND = jnp.bfloat16
VMEM = 24
UNROLL = True


ORDERS = ((0, 1, 3, 2), (0, 3, 1, 2))


def slot_of(section, z):
    apart = ((section >> 1) - (z >> 1)) & 3
    pair = jnp.where(apart == 0, 0, jnp.where(apart == 3, 1, apart + 1))
    return 2 * pair + ((section ^ z) & 1)


def image_step(sides, sections, side, share, place, stream, cotangent, *refs):
    gathered, refs = refs[:12], refs[12:]
    outs, refs = refs[:4], refs[4:]
    x_in, d_in, w_all, g_all, saved_p, slopes, fwd_pad, bwd_pad, line_pad, x_sem, w_sem, g_sem = refs
    z, x, y, core = place[0], place[1], place[2], place[3]
    channels = stream.shape[-1]
    pixels = side * side
    rows = w_all.shape[1]
    half = rows // 2
    slots = sections // 2
    x_copy = pltpu.make_async_copy(stream, x_in, x_sem.at[0])
    d_copy = pltpu.make_async_copy(cotangent, d_in, x_sem.at[1])

    def lines(role, first, second):
        px = x ^ jnp.where(role == 0, second, first)
        py = y ^ jnp.where(role == 0, first, second)
        start = pl.multiple_of(((px * sides + py) * 2 + role) * share, 8)
        return pl.ds(start, share)

    copies = []
    for which in range(2):
        role = core if which == 0 else 1 - core
        for part in range(2):
            near, one, two = gathered[6 * which + 3 * part : 6 * which + 3 * part + 3]
            for i in range(sides):
                for j, source in enumerate((near.at[i], one.at[i], two.at[0, i], two.at[1, i])):
                    where = lines(role, ORDERS[part][i], ORDERS[part][j])
                    target = w_all.at[pl.ds(part * slots, slots), where, :]
                    copies.append(pltpu.make_async_copy(source, target, w_sem.at[len(copies)]))

    def send(slot):
        part, place_in = slot // slots, lax.rem(slot, slots)
        for a, role in enumerate((1 - core, core)):
            for j in (2, 3, 0, 1):
                which = 2 * a + (1 if j < 2 else 0)
                second = jnp.where(part == 0, ORDERS[0][j], ORDERS[1][j])
                for i in range(sides):
                    first = jnp.where(part == 0, ORDERS[0][i], ORDERS[1][i])
                    source = g_all.at[slot, lines(role, first, second), :]
                    target = outs[which].at[part, j % 2, i, place_in]
                    pltpu.make_async_copy(source, target, g_sem.at[which]).start()

    x_copy.start()
    for copy in copies:
        copy.start()
    d_copy.start()
    edge = jnp.zeros((side, 3 * channels), ROUND)
    for pad in (fwd_pad, bwd_pad):
        for k in range(2):
            pad[k, 0:side, :] = edge
            pad[k, side + pixels : 2 * side + pixels, :] = edge

    column = lax.broadcasted_iota(jnp.int32, (pixels, channels), 0) & (side - 1)
    not_first = column > 0
    not_last = column < side - 1

    def around(v):
        line_pad[8 : 8 + pixels, :] = v
        low = jnp.where(not_first, line_pad[7 : 7 + pixels, :], 0.0).astype(ROUND)
        high = jnp.where(not_last, line_pad[9 : 9 + pixels, :], 0.0).astype(ROUND)
        return low, high

    def band(pad, k, low, mid, high):
        body = pl.ds(side, pixels)
        pad[k, body, 0:channels] = low
        pad[k, body, channels : 2 * channels] = mid
        pad[k, body, 2 * channels : 3 * channels] = high

    def conv(pad, k, w):
        taps = jnp.concatenate([pad[k, a * side : a * side + pixels, :] for a in range(3)], axis=1)
        return jnp.dot(taps, w, preferred_element_type=jnp.float32)

    def activate(v, at):
        logistic = 1.0 / (1.0 + jnp.exp(-v))
        p = v * logistic
        slopes[at] = logistic + p * (1.0 - logistic)
        saved_p[at] = p.T.astype(ROUND)
        return p

    def forward(s, pair):
        x1, x2 = pair
        w = w_all.at[slot_of(s, z)]
        p = activate(x2, 2 * s)
        low, high = around(p)
        band(fwd_pad, 0, low, p.astype(ROUND), high)
        y1 = x1 + conv(fwd_pad, 0, w[0:half, :])
        p = activate(y1, 2 * s + 1)
        low, high = around(p)
        band(fwd_pad, 1, low, p.astype(ROUND), high)
        y2 = x2 + conv(fwd_pad, 1, w[half:rows, :])
        return y1, y2

    x_copy.wait()
    for copy in copies:
        copy.wait()
    lax.fori_loop(0, sections, forward, (x_in[0], x_in[1]), unroll=UNROLL)

    def spread(k, e, w, g, base, at):
        low, high = around(e)
        band(bwd_pad, k, high, e.astype(ROUND), low)
        total = None
        pieces = []
        for a in range(3):
            lines = bwd_pad[k, (2 - a) * side : (2 - a) * side + pixels, :]
            pieces.append(lines)
            for b in range(3):
                first = base + (3 * a + b) * channels
                part = lax.dot_general(
                    lines[:, b * channels : (b + 1) * channels], w[first : first + channels, :],
                    (((1,), (1,)), ((), ())), preferred_element_type=jnp.float32,
                )
                total = part if total is None else total + part
        wgrad = jnp.dot(
            saved_p[at], jnp.concatenate(pieces, axis=1), preferred_element_type=jnp.float32
        ).astype(ROUND)
        for tap in range(9):
            first = base + tap * channels
            g[first : first + channels, :] = wgrad[:, tap * channels : (tap + 1) * channels]
        return total * slopes[at]

    def backward(step, pair):
        d1, d2 = pair
        s = sections - 1 - step
        slot = slot_of(s, z)
        w = w_all.at[slot]
        g = g_all.at[slot]
        d1 = d1 + spread(0, d2, w, g, half, 2 * s + 1)
        d2 = d2 + spread(1, d1, w, g, 0, 2 * s)
        send(slot)
        return d1, d2

    d_copy.wait()
    lax.fori_loop(0, sections, backward, (d_in[0], d_in[1]), unroll=UNROLL)
    for which, out in enumerate(outs):
        pltpu.make_async_copy(out, out, g_sem.at[which]).wait()


def image_grads(stream, cotangent, gathered, place, sides):
    pixels, channels = stream.shape[1:]
    side = int(round(pixels**0.5))
    share = gathered[0].shape[2]
    sections = 2 * gathered[0].shape[1]
    rows = share * 2 * sides * sides
    far = pl.BlockSpec(memory_space=pl.ANY)
    kernel = lambda *refs: image_step(sides, sections, side, share, *refs)
    piece = (2, 2, sides, sections // 2, share, channels)
    return pl.pallas_call(
        kernel,
        out_shape=[jax.ShapeDtypeStruct(piece, ROUND)] * 4,
        grid_spec=pltpu.PrefetchScalarGridSpec(
            num_scalar_prefetch=1,
            grid=(1,),
            in_specs=[far] * 14,
            out_specs=[far] * 4,
            scratch_shapes=[
                pltpu.VMEM((2, pixels, channels), jnp.float32),
                pltpu.VMEM((2, pixels, channels), jnp.float32),
                pltpu.VMEM((sections, rows, channels), ROUND),
                pltpu.VMEM((sections, rows, channels), ROUND),
                pltpu.VMEM((2 * sections, channels, pixels), ROUND),
                pltpu.VMEM((2 * sections, pixels, channels), jnp.float32),
                pltpu.VMEM((2, pixels + 2 * side, 3 * channels), ROUND),
                pltpu.VMEM((2, pixels + 2 * side, 3 * channels), ROUND),
                pltpu.VMEM((pixels + 16, channels), jnp.float32),
                pltpu.SemaphoreType.DMA((2,)),
                pltpu.SemaphoreType.DMA((4 * sides * sides,)),
                pltpu.SemaphoreType.DMA((4,)),
            ],
        ),
        compiler_params=pltpu.CompilerParams(vmem_limit_bytes=VMEM << 20),
        name="image_step",
    )(place, stream, cotangent, *gathered)


def crossed_z(value):
    n = lax.axis_size("section")
    return lax.ppermute(value, "section", [(i, i ^ 1) for i in range(n)])


def moved_z(value, by):
    n = lax.axis_size("section")
    return lax.ppermute(value, "section", [(i, (i + by) % n) for i in range(n)])


def in_plane(sides, value, to):
    pairs = []
    for x in range(sides):
        for y in range(sides):
            for core in range(2):
                px, py, pc = to(x, y, core)
                pairs.append(((x * sides + y) * 2 + core, (px * sides + py) * 2 + pc))
    return lax.ppermute(value, "dp", pairs)


def along_first(sides, value, mask):
    return in_plane(sides, value, lambda x, y, c: (x, y ^ mask, c) if c == 0 else (x ^ mask, y, c))


def along_second(sides, value, mask):
    return in_plane(sides, value, lambda x, y, c: (x ^ mask, y, c) if c == 0 else (x, y ^ mask, c))


def swapped(sides, value):
    return in_plane(sides, value, lambda x, y, c: (x, y, 1 - c))


def gather_weights(mine, sides):
    pair = jnp.stack([mine, crossed_z(mine)])
    below = moved_z(pair, 2)
    above = moved_z(pair, -2)
    across = moved_z(below, 2)
    own = []
    lines = [jnp.concatenate([pair, below])[None], jnp.concatenate([above, across])[None]]
    for turn in range(2):
        for part in range(2):
            got = along_first(sides, lines[part], (1, 3)[turn ^ part])
            lines[part] = jnp.concatenate([lines[part], got])
    one = [along_second(sides, lines[part], (1, 3)[part]) for part in range(2)]
    two = [along_second(sides, jnp.stack([lines[part], one[part]]), (3, 1)[part]) for part in range(2)]
    own = [lines[0], one[0], two[0], lines[1], one[1], two[1]]
    return own + [swapped(sides, block) for block in own]


def wide(value):
    return value.astype(jnp.float32)


def scatter_grads(blocks, sides):
    passed_far, passed_near, kept_far, kept_near = blocks
    far = swapped(sides, passed_far)
    near = swapped(sides, passed_near)
    came = []
    for part in range(2):
        out = (wide(kept_far[part]) + wide(far[part])).astype(ROUND)
        came.append(along_second(sides, out, (3, 1)[part]))
    lines = []
    for part in range(2):
        out = (wide(kept_near[part, 1]) + wide(near[part, 1]) + wide(came[part][1])).astype(ROUND)
        last = along_second(sides, out, (1, 3)[part])
        lines.append(wide(kept_near[part, 0]) + wide(near[part, 0]) + wide(came[part][0]) + wide(last))
    for turn in range(2):
        for part in range(2):
            line = lines[part]
            middle = line.shape[0] // 2
            got = along_first(sides, line[middle:].astype(ROUND), (3, 1)[turn ^ part])
            lines[part] = line[:middle] + wide(got)
    (here, below), (above, across) = (jnp.split(line[0], 2) for line in lines)
    below = below + wide(moved_z(across.astype(ROUND), -2))
    here = here + wide(moved_z(above.astype(ROUND), 2)) + wide(moved_z(below.astype(ROUND), -2))
    return here[0] + wide(crossed_z(here[1].astype(ROUND)))


def on_device(stream, cotangent, weights, master, momentum):
    dp = lax.axis_size("dp")
    sides = int(round((dp // 2) ** 0.5))
    images = stream.shape[1] * dp
    share = weights.shape[1] // dp
    channels = weights.shape[2]
    z, at = lax.axis_index("section"), lax.axis_index("dp")
    place = jnp.stack([z, at // (2 * sides), at // 2 % sides, at % 2]).astype(jnp.int32)
    mine = lax.dynamic_slice_in_dim(weights[0], at * share, share, 0)
    gathered = gather_weights(mine, sides)
    pair = (2, stream.shape[2] * stream.shape[3], channels)
    first, last = (lax.dynamic_slice_in_dim(v, z, 1, 1).reshape(pair) for v in (stream, cotangent))
    blocks = image_grads(first, last, gathered, place, sides)
    gradient = scatter_grads(blocks, sides) / images
    new_momentum = INERTIA * momentum[0] + gradient
    new_master = master[0] - STEP_SIZE * new_momentum
    copies = jnp.broadcast_to(new_master.astype(ROUND)[None], (dp, share, channels))
    new_weights = lax.all_to_all(copies, "dp", 0, 0, tiled=True).reshape(dp * share, channels)
    return (new_master[None], new_momentum[None], new_weights[None])


def solution(mesh):
    placed = (
        P(None, "dp", None, None, None),
        P(None, "dp", None, None, None),
        P("section", None, None),
        P("section", "dp", None),
        P("section", "dp", None),
    )
    return jax.shard_map(
        on_device,
        mesh=mesh,
        in_specs=placed,
        out_specs=(P("section", "dp", None), P("section", "dp", None), P("section", None, None)),
        check_vma=False,
    )
```

```python
import jax
import jax.numpy as jnp
from jax import lax
from jax.experimental import pallas as pl
from jax.experimental.pallas import tpu as pltpu
from jax.sharding import PartitionSpec as P

STEP_SIZE = 0.1
INERTIA = 0.9
ROUND = jnp.bfloat16
VMEM = 24


ORDERS = ((0, 1, 3, 2), (0, 3, 1, 2))


def rank_in(part, distance):
    if part == 0:
        return distance ^ (distance >> 1)
    return ((distance << 1) & 3) ^ (3 * (distance >> 1))


def block_table(sides, x, y, core):
    block = jnp.arange(2 * sides * sides)
    role = block % 2
    px, py = (block // (2 * sides)) ^ x, (block // 2 % sides) ^ y
    first, second = jnp.where(role == 0, py, px), jnp.where(role == 0, px, py)
    stays = (role == core).astype(jnp.int32)
    tables = []
    for part in range(2):
        rank = rank_in(part, second)
        late = 1 - rank // 2
        tables.append((((stays * 2 + late) * 2 + part) * 2 + rank % 2) * sides + first)
    return jnp.concatenate(tables).astype(jnp.int32)


def slot_of(section, z):
    apart = ((section >> 1) - (z >> 1)) & 3
    pair = jnp.where(apart == 0, 0, jnp.where(apart == 3, 1, apart + 1))
    return 2 * pair + ((section ^ z) & 1)


def image_step(sides, sections, side, share, place, table, stream, cotangent, *refs):
    gathered, refs = refs[:12], refs[12:]
    out, refs = refs[0], refs[1:]
    x_in, d_in, w_all, saved_p, slopes, fwd_pad, bwd_pad, line_pad, x_sem, w_sem = refs
    z, x, y, core = place[0], place[1], place[2], place[3]
    channels = stream.shape[-1]
    pixels = side * side
    rows = w_all.shape[1]
    half = rows // 2
    slots = sections // 2
    blocks = 2 * sides * sides
    x_copy = pltpu.make_async_copy(stream, x_in, x_sem.at[0])
    d_copy = pltpu.make_async_copy(cotangent, d_in, x_sem.at[1])

    def lines(role, first, second):
        px = x ^ jnp.where(role == 0, second, first)
        py = y ^ jnp.where(role == 0, first, second)
        start = pl.multiple_of(((px * sides + py) * 2 + role) * share, 8)
        return pl.ds(start, share)

    copies = []
    for which in range(2):
        role = core if which == 0 else 1 - core
        for part in range(2):
            near, one, two = gathered[6 * which + 3 * part : 6 * which + 3 * part + 3]
            for i in range(sides):
                for j, source in enumerate((near.at[i], one.at[i], two.at[0, i], two.at[1, i])):
                    where = lines(role, i, ORDERS[part][j])
                    target = w_all.at[pl.ds(part * slots, slots), where, :]
                    copies.append(pltpu.make_async_copy(source, target, w_sem.at[len(copies)]))

    x_copy.start()
    for copy in copies:
        copy.start()
    d_copy.start()
    edge = jnp.zeros((side, 3 * channels), ROUND)
    for pad in (fwd_pad, bwd_pad):
        for k in range(2):
            pad[k, 0:side, :] = edge
            pad[k, side + pixels : 2 * side + pixels, :] = edge

    column = lax.broadcasted_iota(jnp.int32, (pixels, channels), 0) & (side - 1)
    not_first = column > 0
    not_last = column < side - 1

    def around(v):
        line_pad[8 : 8 + pixels, :] = v
        low = jnp.where(not_first, line_pad[7 : 7 + pixels, :], 0.0).astype(ROUND)
        high = jnp.where(not_last, line_pad[9 : 9 + pixels, :], 0.0).astype(ROUND)
        return low, high

    def band(pad, k, low, mid, high):
        body = pl.ds(side, pixels)
        pad[k, body, 0:channels] = low
        pad[k, body, channels : 2 * channels] = mid
        pad[k, body, 2 * channels : 3 * channels] = high

    def conv(pad, k, w):
        taps = jnp.concatenate([pad[k, a * side : a * side + pixels, :] for a in range(3)], axis=1)
        return jnp.dot(taps, w, preferred_element_type=jnp.float32)

    def activate(v, at):
        logistic = 1.0 / (1.0 + jnp.exp(-v))
        p = v * logistic
        slopes[at] = logistic + p * (1.0 - logistic)
        saved_p[at] = p.T.astype(ROUND)
        return p

    def forward(s, pair):
        x1, x2 = pair
        w = w_all.at[slot_of(s, z)]
        p = activate(x2, 2 * s)
        low, high = around(p)
        band(fwd_pad, 0, low, p.astype(ROUND), high)
        y1 = x1 + conv(fwd_pad, 0, w[0:half, :])
        p = activate(y1, 2 * s + 1)
        low, high = around(p)
        band(fwd_pad, 1, low, p.astype(ROUND), high)
        y2 = x2 + conv(fwd_pad, 1, w[half:rows, :])
        return y1, y2

    x_copy.wait()
    for copy in copies:
        copy.wait()
    lax.fori_loop(0, sections, forward, (x_in[0], x_in[1]), unroll=True)

    def spread(k, e, w, s, base, at):
        low, high = around(e)
        band(bwd_pad, k, high, e.astype(ROUND), low)
        taps = jnp.concatenate(
            [bwd_pad[k, (2 - a) * side : (2 - a) * side + pixels, :] for a in range(3)], axis=1
        )
        across = jnp.concatenate(
            [w[base + tap * channels : base + (tap + 1) * channels, :] for tap in range(9)], axis=1
        )
        total = lax.dot_general(taps, across, (((1,), (1,)), ((), ())), preferred_element_type=jnp.float32)
        wgrad = jnp.dot(saved_p[at], taps, preferred_element_type=jnp.float32)
        for tap in range(9):
            row, end = base + tap * channels, base + (tap + 1) * channels
            while row < end:
                block = row // share
                stop = min(end, (block + 1) * share)
                n = table[s // slots * blocks + block] * slots + s % slots
                c = row - base - tap * channels
                piece = wgrad[c : c + stop - row, tap * channels : (tap + 1) * channels].astype(ROUND)
                out[n, row - block * share : stop - block * share, :] = piece
                row = stop
        return total * slopes[at]

    def backward(step, pair):
        d1, d2 = pair
        s = sections - 1 - step
        w = w_all.at[slot_of(s, z)]
        d1 = d1 + spread(0, d2, w, s, half, 2 * s + 1)
        d2 = d2 + spread(1, d1, w, s, 0, 2 * s)
        return d1, d2

    d_copy.wait()
    pair = d_in[0], d_in[1]
    for step in range(sections):
        pair = backward(step, pair)


def image_grads(stream, cotangent, gathered, place, table, sides):
    pixels, channels = stream.shape[1:]
    side = int(round(pixels**0.5))
    share = gathered[0].shape[2]
    sections = 2 * gathered[0].shape[1]
    rows = share * 2 * sides * sides
    far = pl.BlockSpec(memory_space=pl.ANY)
    kernel = lambda *refs: image_step(sides, sections, side, share, *refs)
    whole = 2 * sides * sides * sections
    return pl.pallas_call(
        kernel,
        out_shape=jax.ShapeDtypeStruct((whole, share, channels), ROUND),
        grid_spec=pltpu.PrefetchScalarGridSpec(
            num_scalar_prefetch=2,
            grid=(1,),
            in_specs=[far] * 14,
            out_specs=pl.BlockSpec(memory_space=pltpu.VMEM),
            scratch_shapes=[
                pltpu.VMEM((2, pixels, channels), jnp.float32),
                pltpu.VMEM((2, pixels, channels), jnp.float32),
                pltpu.VMEM((sections, rows, channels), ROUND),
                pltpu.VMEM((2 * sections, channels, pixels), ROUND),
                pltpu.VMEM((2 * sections, pixels, channels), jnp.float32),
                pltpu.VMEM((2, pixels + 2 * side, 3 * channels), ROUND),
                pltpu.VMEM((2, pixels + 2 * side, 3 * channels), ROUND),
                pltpu.VMEM((pixels + 16, channels), jnp.float32),
                pltpu.SemaphoreType.DMA((2,)),
                pltpu.SemaphoreType.DMA((4 * sides * sides,)),
            ],
        ),
        compiler_params=pltpu.CompilerParams(vmem_limit_bytes=VMEM << 20),
        name="image_step",
    )(place, table, stream, cotangent, *gathered)


def crossed_z(value):
    n = lax.axis_size("section")
    return lax.ppermute(value, "section", [(i, i ^ 1) for i in range(n)])


def moved_z(value, by):
    n = lax.axis_size("section")
    return lax.ppermute(value, "section", [(i, (i + by) % n) for i in range(n)])


def in_plane(sides, value, to):
    pairs = []
    for x in range(sides):
        for y in range(sides):
            for core in range(2):
                px, py, pc = to(x, y, core)
                pairs.append(((x * sides + y) * 2 + core, (px * sides + py) * 2 + pc))
    return lax.ppermute(value, "dp", pairs)


def along_first(sides, value, mask):
    return in_plane(sides, value, lambda x, y, c: (x, y ^ mask, c) if c == 0 else (x ^ mask, y, c))


def along_second(sides, value, mask):
    return in_plane(sides, value, lambda x, y, c: (x ^ mask, y, c) if c == 0 else (x, y ^ mask, c))


def swapped(sides, value):
    return in_plane(sides, value, lambda x, y, c: (x, y, 1 - c))


def gather_weights(mine, sides):
    pair = jnp.stack([mine, crossed_z(mine)])
    below = moved_z(pair, 2)
    above = moved_z(pair, -2)
    across = moved_z(below, 2)
    line = jnp.stack([jnp.concatenate([pair, below]), jnp.concatenate([above, across])])
    came = [line] + [along_first(sides, line, mask) for mask in range(1, sides)]
    lines = [jnp.stack([got[part] for got in came]) for part in range(2)]
    one = [along_second(sides, lines[part], (1, 3)[part]) for part in range(2)]
    two = [along_second(sides, jnp.stack([lines[part], one[part]]), (3, 1)[part]) for part in range(2)]
    own = [lines[0], one[0], two[0], lines[1], one[1], two[1]]
    return own + [swapped(sides, block) for block in own]


def wide(value):
    return value.astype(jnp.float32)


def scatter_grads(blocks, sides):
    (passed_far, passed_near), (kept_far, kept_near) = blocks
    far = swapped(sides, passed_far)
    near = swapped(sides, passed_near)
    came = []
    for part in range(2):
        out = (wide(kept_far[part]) + wide(far[part])).astype(ROUND)
        came.append(along_second(sides, out, (3, 1)[part]))
    lines = []
    for part in range(2):
        out = (wide(kept_near[part, 1]) + wide(near[part, 1]) + wide(came[part][1])).astype(ROUND)
        last = along_second(sides, out, (1, 3)[part])
        lines.append(wide(kept_near[part, 0]) + wide(near[part, 0]) + wide(came[part][0]) + wide(last))
    line = jnp.concatenate(lines, axis=1)
    total = line[0]
    line = line.astype(ROUND)
    for mask in range(1, sides):
        total = total + wide(along_first(sides, line[mask], mask))
    tiles = lax.all_to_all(total.astype(ROUND), "section", 0, 0, tiled=True)
    return jnp.sum(wide(tiles), axis=0)


def on_device(stream, cotangent, weights, master, momentum):
    dp = lax.axis_size("dp")
    sides = int(round((dp // 2) ** 0.5))
    images = stream.shape[1] * dp
    share = weights.shape[1] // dp
    channels = weights.shape[2]
    z, at = lax.axis_index("section"), lax.axis_index("dp")
    place = jnp.stack([z, at // (2 * sides), at // 2 % sides, at % 2]).astype(jnp.int32)
    mine = lax.dynamic_slice_in_dim(weights[0], at * share, share, 0)
    gathered = gather_weights(mine, sides)
    pair = (2, stream.shape[2] * stream.shape[3], channels)
    first, last = (lax.dynamic_slice_in_dim(v, z, 1, 1).reshape(pair) for v in (stream, cotangent))
    table = block_table(sides, *place[1:])
    blocks = image_grads(first, last, gathered, place, table, sides)
    blocks = blocks.reshape(2, 2, 2, 2, sides, -1, share, channels)
    gradient = scatter_grads(blocks, sides) / images
    new_momentum = INERTIA * momentum[0] + gradient
    new_master = master[0] - STEP_SIZE * new_momentum
    copies = jnp.broadcast_to(new_master.astype(ROUND)[None], (dp, share, channels))
    new_weights = lax.all_to_all(copies, "dp", 0, 0, tiled=True).reshape(dp * share, channels)
    return (new_master[None], new_momentum[None], new_weights[None])


def solution(mesh):
    placed = (
        P(None, "dp", None, None, None),
        P(None, "dp", None, None, None),
        P("section", None, None),
        P("section", "dp", None),
        P("section", "dp", None),
    )
    return jax.shard_map(
        on_device,
        mesh=mesh,
        in_specs=placed,
        out_specs=(P("section", "dp", None), P("section", "dp", None), P("section", None, None)),
        check_vma=False,
    )
```

```python
import jax
import jax.numpy as jnp
from jax import lax
from jax.experimental import pallas as pl
from jax.experimental.pallas import tpu as pltpu
from jax.sharding import PartitionSpec as P

STEP_SIZE = 0.1
INERTIA = 0.9
ROUND = jnp.bfloat16
VMEM = 24
SMALL = 16


ORDERS = ((0, 1, 3, 2), (0, 3, 1, 2))


def rank_in(part, distance):
    if part == 0:
        return distance ^ (distance >> 1)
    return ((distance << 1) & 3) ^ (3 * (distance >> 1))


def block_table(sides, x, y, core):
    block = jnp.arange(2 * sides * sides)
    role = block % 2
    px, py = (block // (2 * sides)) ^ x, (block // 2 % sides) ^ y
    first, second = jnp.where(role == 0, py, px), jnp.where(role == 0, px, py)
    stays = (role == core).astype(jnp.int32)
    tables = []
    for part in range(2):
        turn = sides - 1 - rank_in(part, second)
        tables.append(((stays * sides + turn) * 2 + part) * sides + first)
    return jnp.concatenate(tables).astype(jnp.int32)


def image_step(sides, sections, side, share, place, table, stream, cotangent, *refs):
    gathered, refs = refs[:16], refs[16:]
    out, refs = refs[0], refs[1:]
    x_in, d_in, w_all, saved_p, slopes, fwd_pad, bwd_pad, line_pad, x_sem, w_sem = refs
    z, x, y, core = place[0], place[1], place[2], place[3]
    channels = stream.shape[-1]
    pixels = side * side
    rows = w_all.shape[1]
    half = rows // 2
    slots = sections // 2
    blocks = 2 * sides * sides
    x_copy = pltpu.make_async_copy(stream, x_in, x_sem.at[0])
    d_copy = pltpu.make_async_copy(cotangent, d_in, x_sem.at[1])

    def lines(role, first, second):
        px = x ^ jnp.where(role == 0, second, first)
        py = y ^ jnp.where(role == 0, first, second)
        start = pl.multiple_of(((px * sides + py) * 2 + role) * share, 8)
        return pl.ds(start, share)

    copies = []
    for which in range(2):
        role = core if which == 0 else 1 - core
        for part in range(2):
            sources = gathered[8 * which + 4 * part : 8 * which + 4 * part + 4]
            for i in range(sides):
                for j in range(sides):
                    source = sources[j].at[i]
                    where = lines(role, i, ORDERS[part][j])
                    target = w_all.at[pl.ds(part * slots, slots), where, :]
                    copies.append(pltpu.make_async_copy(source, target, w_sem.at[len(copies)]))

    x_copy.start()
    for copy in copies:
        copy.start()
    d_copy.start()
    edge = jnp.zeros((side, 3 * channels), ROUND)
    for pad in (fwd_pad, bwd_pad):
        for k in range(2):
            pad[k, 0:side, :] = edge
            pad[k, side + pixels : 2 * side + pixels, :] = edge

    column = lax.broadcasted_iota(jnp.int32, (pixels, channels), 0) & (side - 1)
    not_first = column > 0
    not_last = column < side - 1

    def around(v):
        line_pad[8 : 8 + pixels, :] = v
        low = jnp.where(not_first, line_pad[7 : 7 + pixels, :], 0.0).astype(ROUND)
        high = jnp.where(not_last, line_pad[9 : 9 + pixels, :], 0.0).astype(ROUND)
        return low, high

    def band(pad, k, low, mid, high):
        body = pl.ds(side, pixels)
        pad[k, body, 0:channels] = low
        pad[k, body, channels : 2 * channels] = mid
        pad[k, body, 2 * channels : 3 * channels] = high

    def conv(pad, k, w):
        taps = jnp.concatenate([pad[k, a * side : a * side + pixels, :] for a in range(3)], axis=1)
        return jnp.dot(taps, w, preferred_element_type=jnp.float32)

    def activate(v, at):
        logistic = 1.0 / (1.0 + jnp.exp(-v))
        p = v * logistic
        slopes[at] = logistic + p * (1.0 - logistic)
        saved_p[at] = p.T.astype(ROUND)
        return p

    def forward(s, pair):
        x1, x2 = pair
        w = w_all.at[s]
        p = activate(x2, 2 * s)
        low, high = around(p)
        band(fwd_pad, 0, low, p.astype(ROUND), high)
        y1 = x1 + conv(fwd_pad, 0, w[0:half, :])
        p = activate(y1, 2 * s + 1)
        low, high = around(p)
        band(fwd_pad, 1, low, p.astype(ROUND), high)
        y2 = x2 + conv(fwd_pad, 1, w[half:rows, :])
        return y1, y2

    x_copy.wait()
    for copy in copies:
        copy.wait()
    lax.fori_loop(0, sections, forward, (x_in[0], x_in[1]), unroll=True)

    def spread(k, e, w, s, base, at):
        low, high = around(e)
        band(bwd_pad, k, high, e.astype(ROUND), low)
        taps = jnp.concatenate(
            [bwd_pad[k, (2 - a) * side : (2 - a) * side + pixels, :] for a in range(3)], axis=1
        )
        across = jnp.concatenate(
            [w[base + tap * channels : base + (tap + 1) * channels, :] for tap in range(9)], axis=1
        )
        total = lax.dot_general(taps, across, (((1,), (1,)), ((), ())), preferred_element_type=jnp.float32)
        wgrad = jnp.dot(saved_p[at], taps, preferred_element_type=jnp.float32)
        for tap in range(9):
            row, end = base + tap * channels, base + (tap + 1) * channels
            while row < end:
                block = row // share
                stop = min(end, (block + 1) * share)
                n = table[s // slots * blocks + block] * slots + s % slots
                c = row - base - tap * channels
                piece = wgrad[c : c + stop - row, tap * channels : (tap + 1) * channels].astype(ROUND)
                out[n, row - block * share : stop - block * share, :] = piece
                row = stop
        return total * slopes[at]

    def backward(step, pair):
        d1, d2 = pair
        s = sections - 1 - step
        w = w_all.at[s]
        d1 = d1 + spread(0, d2, w, s, half, 2 * s + 1)
        d2 = d2 + spread(1, d1, w, s, 0, 2 * s)
        return d1, d2

    d_copy.wait()
    pair = d_in[0], d_in[1]
    for step in range(sections):
        pair = backward(step, pair)


def image_grads(stream, cotangent, gathered, place, table, sides):
    pixels, channels = stream.shape[1:]
    side = int(round(pixels**0.5))
    share = gathered[0].shape[2]
    sections = 2 * gathered[0].shape[1]
    rows = share * 2 * sides * sides
    far = pl.BlockSpec(memory_space=pl.ANY)
    kernel = lambda *refs: image_step(sides, sections, side, share, *refs)
    whole = 2 * sides * sides * sections
    return pl.pallas_call(
        kernel,
        out_shape=jax.ShapeDtypeStruct((whole, share, channels), ROUND),
        grid_spec=pltpu.PrefetchScalarGridSpec(
            num_scalar_prefetch=2,
            grid=(1,),
            in_specs=[far] * 18,
            out_specs=pl.BlockSpec(memory_space=pltpu.VMEM),
            scratch_shapes=[
                pltpu.VMEM((2, pixels, channels), jnp.float32),
                pltpu.VMEM((2, pixels, channels), jnp.float32),
                pltpu.VMEM((sections, rows, channels), ROUND),
                pltpu.VMEM((2 * sections, channels, pixels), ROUND),
                pltpu.VMEM((2 * sections, pixels, channels), jnp.float32),
                pltpu.VMEM((2, pixels + 2 * side, 3 * channels), ROUND),
                pltpu.VMEM((2, pixels + 2 * side, 3 * channels), ROUND),
                pltpu.VMEM((pixels + 16, channels), jnp.float32),
                pltpu.SemaphoreType.DMA((2,)),
                pltpu.SemaphoreType.DMA((4 * sides * sides,)),
            ],
        ),
        compiler_params=pltpu.CompilerParams(vmem_limit_bytes=VMEM << 20),
        name="image_step",
    )(place, table, stream, cotangent, *gathered)


def in_plane(sides, value, to):
    pairs = []
    for x in range(sides):
        for y in range(sides):
            for core in range(2):
                px, py, pc = to(x, y, core)
                pairs.append(((x * sides + y) * 2 + core, (px * sides + py) * 2 + pc))
    return lax.ppermute(value, "dp", pairs)


def along_first(sides, value, mask):
    return in_plane(sides, value, lambda x, y, c: (x, y ^ mask, c) if c == 0 else (x ^ mask, y, c))


def along_second(sides, value, mask):
    return in_plane(sides, value, lambda x, y, c: (x ^ mask, y, c) if c == 0 else (x, y ^ mask, c))


def swapped(sides, value):
    return in_plane(sides, value, lambda x, y, c: (x, y, 1 - c))


def gather_weights(mine, early, sides):
    sections = lax.axis_size("section")
    line = jnp.broadcast_to(mine, (sections, *mine.shape))
    line = lax.all_to_all(line, "section", 0, 0, tiled=True).reshape(2, -1, *mine.shape)
    came = [line] + [along_first(sides, line, mask) for mask in range(1, sides)]
    lines = [jnp.stack([got[part] for got in came]) for part in range(2)]
    wait = sum(nothing(value[0, : mine.shape[0]]) for value in early).astype(ROUND)
    lines = [block + wait for block in lines]
    with jax.named_scope("get_one"):
        one = [along_second(sides, lines[part], ORDERS[part][1]) for part in range(2)]
    with jax.named_scope("get_three"):
        three = [along_second(sides, lines[part], ORDERS[part][2]) for part in range(2)]
    with jax.named_scope("get_two"):
        two = [along_second(sides, one[part], ORDERS[part][2]) for part in range(2)]
    own = [block for part in range(2) for block in (lines[part], one[part], three[part], two[part])]
    with jax.named_scope("share"):
        theirs = []
        for part in range(2):
            line = lines[part] + nothing(one[part]).astype(ROUND)
            theirs += [swapped(sides, block) for block in (line, one[part], three[part], two[part])]
    return own + theirs


def nothing(value):
    return jnp.minimum(jnp.abs(value.astype(jnp.float32)), 0.0)


def wide(value):
    return value.astype(jnp.float32)


def added(blocks, which, swap, *came):
    first = which[0][0]

    def kernel(blocks, swap, *refs):
        for at, (turn, part) in enumerate(which):
            total = wide(blocks[1, turn, part]) + wide(swap[turn - first, part])
            if came:
                total = total + wide(refs[at][...])
            refs[len(came) + at][...] = total.astype(ROUND)

    near = pl.BlockSpec(memory_space=pltpu.VMEM)
    return pl.pallas_call(
        kernel,
        out_shape=[jax.ShapeDtypeStruct(blocks.shape[3:], ROUND)] * len(which),
        in_specs=[near] * (2 + len(came)),
        out_specs=[near] * len(which),
        compiler_params=pltpu.CompilerParams(vmem_limit_bytes=SMALL << 20),
        name="added",
    )(blocks, swap, *came)


def scatter_grads(blocks, sides):
    passed = blocks[0]
    with jax.named_scope("swap_far"):
        far = swapped(sides, passed[:2])
    with jax.named_scope("swap_near"):
        near = swapped(sides, passed[2:])
    two, three, one = [None] * 2, [None] * 2, [None] * 2
    two[0], two[1], three[0], three[1] = added(blocks, ((0, 0), (0, 1), (1, 0), (1, 1)), far)
    for part in range(2):
        with jax.named_scope("sum_two"):
            two[part] = along_second(sides, two[part], ORDERS[part][2])
    for part in range(2):
        with jax.named_scope("sum_three"):
            three[part] = along_second(sides, three[part], ORDERS[part][2])
    one = list(added(blocks, ((2, 0), (2, 1)), near, *two))
    for part in range(2):
        with jax.named_scope("sum_one"):
            one[part] = along_second(sides, one[part], ORDERS[part][1])
    lines = []
    for part in range(2):
        lines.append(wide(blocks[1, 3, part]) + wide(near[1, part]) + wide(three[part]) + wide(one[part]))
    line = jnp.concatenate(lines, axis=1)
    total = line[0]
    line = line.astype(ROUND)
    for mask in range(1, sides):
        total = total + wide(along_first(sides, line[mask], mask))
    tiles = lax.all_to_all(total.astype(ROUND), "section", 0, 0, tiled=True)
    return jnp.sum(wide(tiles), axis=0)


def on_device(stream, cotangent, weights, master, momentum):
    dp = lax.axis_size("dp")
    sides = int(round((dp // 2) ** 0.5))
    images = stream.shape[1] * dp
    share = weights.shape[1] // dp
    channels = weights.shape[2]
    z, at = lax.axis_index("section"), lax.axis_index("dp")
    place = jnp.stack([z, at // (2 * sides), at // 2 % sides, at % 2]).astype(jnp.int32)
    mine = lax.dynamic_slice_in_dim(weights[0], at * share, share, 0)
    pair = (2, stream.shape[2] * stream.shape[3], channels)
    first, last = (lax.dynamic_slice_in_dim(v, z, 1, 1).reshape(pair) for v in (stream, cotangent))
    gathered = gather_weights(mine, (first, last), sides)
    table = block_table(sides, *place[1:])
    blocks = image_grads(first, last, gathered, place, table, sides)
    blocks = blocks.reshape(2, sides, 2, sides, -1, share, channels)
    gradient = scatter_grads(blocks, sides) / images
    new_momentum = INERTIA * momentum[0] + gradient
    new_master = master[0] - STEP_SIZE * new_momentum
    chips = dp // 2
    copies = jnp.broadcast_to(new_master.astype(ROUND)[None], (chips, share, channels))
    same_core = [[2 * chip + core for chip in range(chips)] for core in range(2)]
    own = lax.all_to_all(copies, "dp", 0, 0, tiled=True, axis_index_groups=same_core)
    other = swapped(sides, own)
    even = (at % 2 == 0)
    both = [jnp.where(even, own, other), jnp.where(even, other, own)]
    new_weights = jnp.stack(both, axis=1).reshape(dp * share, channels)
    return (new_master[None], new_momentum[None], new_weights[None])


def solution(mesh):
    placed = (
        P(None, "dp", None, None, None),
        P(None, "dp", None, None, None),
        P("section", None, None),
        P("section", "dp", None),
        P("section", "dp", None),
    )
    return jax.shard_map(
        on_device,
        mesh=mesh,
        in_specs=placed,
        out_specs=(P("section", "dp", None), P("section", "dp", None), P("section", None, None)),
        check_vma=False,
    )
```

```python
import jax
import jax.numpy as jnp
from jax import lax
from jax.experimental import pallas as pl
from jax.experimental.pallas import tpu as pltpu
from jax.sharding import PartitionSpec as P

STEP_SIZE = 0.1
INERTIA = 0.9
ROUND = jnp.bfloat16
VMEM = 24
SMALL = 16


ORDERS = ((0, 1, 3, 2), (0, 3, 1, 2))


def rank_in(part, distance):
    if part == 0:
        return distance ^ (distance >> 1)
    return ((distance << 1) & 3) ^ (3 * (distance >> 1))


def block_table(sides, x, y, core):
    block = jnp.arange(2 * sides * sides)
    role = block % 2
    px, py = (block // (2 * sides)) ^ x, (block // 2 % sides) ^ y
    first, second = jnp.where(role == 0, py, px), jnp.where(role == 0, px, py)
    stays = (role == core).astype(jnp.int32)
    tables = []
    for part in range(2):
        turn = sides - 1 - rank_in(part, second)
        tables.append(((stays * sides + turn) * 2 + part) * sides + first)
    return jnp.concatenate(tables).astype(jnp.int32)


def in_strips(value, product):
    return jnp.concatenate([product(part) for part in jnp.split(value, 2)], axis=0)


def image_step(sides, sections, side, share, place, table, stream, cotangent, *refs):
    gathered, refs = refs[:8], refs[8:]
    out, refs = refs[0], refs[1:]
    x_in, d_in, w_all, saved_p, slopes, fwd_pad, bwd_pad, line_pad, x_sem, w_sem = refs
    z, x, y, core = place[0], place[1], place[2], place[3]
    channels = stream.shape[-1]
    pixels = side * side
    rows = w_all.shape[1]
    half = rows // 2
    slots = sections // 2
    blocks = 2 * sides * sides
    x_copy = pltpu.make_async_copy(stream, x_in, x_sem.at[0])
    d_copy = pltpu.make_async_copy(cotangent, d_in, x_sem.at[1])

    def lines(role, first, second):
        px = x ^ jnp.where(role == 0, second, first)
        py = y ^ jnp.where(role == 0, first, second)
        start = pl.multiple_of(((px * sides + py) * 2 + role) * share, 8)
        return pl.ds(start, share)

    copies = []
    for part in range(2):
        for which, role in ((0, core), (4, 1 - core)):
            early, late = gathered[which + part], gathered[which + 2 + part]
            sources = early.at[0], early.at[1], late.at[0], late.at[1]
            for i in range(sides):
                for j in range(sides):
                    where = lines(role, i, ORDERS[part][j])
                    target = w_all.at[pl.ds(part * slots, slots), where, :]
                    copies.append(pltpu.make_async_copy(sources[j].at[i], target, w_sem.at[len(copies)]))

    x_copy.start()
    for copy in copies:
        copy.start()
    d_copy.start()
    edge = jnp.zeros((side, 3 * channels), ROUND)
    for pad in (fwd_pad, bwd_pad):
        for k in range(2):
            pad[k, 0:side, :] = edge
            pad[k, side + pixels : 2 * side + pixels, :] = edge

    column = lax.broadcasted_iota(jnp.int32, (pixels, channels), 0) & (side - 1)
    not_first = column > 0
    not_last = column < side - 1

    def around(v):
        line_pad[8 : 8 + pixels, :] = v
        low = jnp.where(not_first, line_pad[7 : 7 + pixels, :], 0.0).astype(ROUND)
        high = jnp.where(not_last, line_pad[9 : 9 + pixels, :], 0.0).astype(ROUND)
        return low, high

    def band(pad, k, low, mid, high):
        body = pl.ds(side, pixels)
        pad[k, body, 0:channels] = low
        pad[k, body, channels : 2 * channels] = mid
        pad[k, body, 2 * channels : 3 * channels] = high

    def conv(pad, k, w):
        taps = jnp.concatenate([pad[k, a * side : a * side + pixels, :] for a in range(3)], axis=1)
        return in_strips(taps, lambda v: jnp.dot(v, w, preferred_element_type=jnp.float32))

    def activate(v, at):
        logistic = 1.0 / (1.0 + jnp.exp(-v))
        p = v * logistic
        slopes[at] = logistic + p * (1.0 - logistic)
        saved_p[at] = p.T.astype(ROUND)
        return p

    def forward(s, pair):
        x1, x2 = pair
        w = w_all.at[s]
        p = activate(x2, 2 * s)
        low, high = around(p)
        band(fwd_pad, 0, low, p.astype(ROUND), high)
        y1 = x1 + conv(fwd_pad, 0, w[0:half, :])
        p = activate(y1, 2 * s + 1)
        low, high = around(p)
        band(fwd_pad, 1, low, p.astype(ROUND), high)
        y2 = x2 + conv(fwd_pad, 1, w[half:rows, :])
        return y1, y2

    x_copy.wait()
    pair = x_in[0], x_in[1]
    for s in range(sections):
        if s % slots == 0:
            for copy in copies[s // slots * len(copies) // 2 : (s // slots + 1) * len(copies) // 2]:
                copy.wait()
        pair = forward(s, pair)

    def spread(k, e, w, s, base, at):
        low, high = around(e)
        band(bwd_pad, k, high, e.astype(ROUND), low)
        taps = jnp.concatenate(
            [bwd_pad[k, (2 - a) * side : (2 - a) * side + pixels, :] for a in range(3)], axis=1
        )
        across = jnp.concatenate(
            [w[base + tap * channels : base + (tap + 1) * channels, :] for tap in range(9)], axis=1
        )
        total = in_strips(
            taps,
            lambda v: lax.dot_general(v, across, (((1,), (1,)), ((), ())), preferred_element_type=jnp.float32),
        )
        wgrad = jnp.dot(saved_p[at], taps, preferred_element_type=jnp.float32)
        for tap in range(9):
            row, end = base + tap * channels, base + (tap + 1) * channels
            while row < end:
                block = row // share
                stop = min(end, (block + 1) * share)
                n = table[s // slots * blocks + block] * slots + s % slots
                c = row - base - tap * channels
                piece = wgrad[c : c + stop - row, tap * channels : (tap + 1) * channels].astype(ROUND)
                out[n, row - block * share : stop - block * share, :] = piece
                row = stop
        return total * slopes[at]

    def backward(step, pair):
        d1, d2 = pair
        s = sections - 1 - step
        w = w_all.at[s]
        d1 = d1 + spread(0, d2, w, s, half, 2 * s + 1)
        d2 = d2 + spread(1, d1, w, s, 0, 2 * s)
        return d1, d2

    d_copy.wait()
    pair = d_in[0], d_in[1]
    for step in range(sections):
        pair = backward(step, pair)


def image_grads(stream, cotangent, gathered, place, table, sides):
    pixels, channels = stream.shape[1:]
    side = int(round(pixels**0.5))
    share = gathered[0].shape[3]
    sections = 2 * gathered[0].shape[2]
    rows = share * 2 * sides * sides
    far = pl.BlockSpec(memory_space=pl.ANY)
    kernel = lambda *refs: image_step(sides, sections, side, share, *refs)
    whole = 2 * sides * sides * sections
    return pl.pallas_call(
        kernel,
        out_shape=jax.ShapeDtypeStruct((whole, share, channels), ROUND),
        grid_spec=pltpu.PrefetchScalarGridSpec(
            num_scalar_prefetch=2,
            grid=(1,),
            in_specs=[far] * 10,
            out_specs=pl.BlockSpec(memory_space=pltpu.VMEM),
            scratch_shapes=[
                pltpu.VMEM((2, pixels, channels), jnp.float32),
                pltpu.VMEM((2, pixels, channels), jnp.float32),
                pltpu.VMEM((sections, rows, channels), ROUND),
                pltpu.VMEM((2 * sections, channels, pixels), ROUND),
                pltpu.VMEM((2 * sections, pixels, channels), jnp.float32),
                pltpu.VMEM((2, pixels + 2 * side, 3 * channels), ROUND),
                pltpu.VMEM((2, pixels + 2 * side, 3 * channels), ROUND),
                pltpu.VMEM((pixels + 16, channels), jnp.float32),
                pltpu.SemaphoreType.DMA((2,)),
                pltpu.SemaphoreType.DMA((4 * sides * sides,)),
            ],
        ),
        compiler_params=pltpu.CompilerParams(vmem_limit_bytes=VMEM << 20),
        name="image_step",
    )(place, table, stream, cotangent, *gathered)


def in_plane(sides, value, to):
    pairs = []
    for x in range(sides):
        for y in range(sides):
            for core in range(2):
                px, py, pc = to(x, y, core)
                pairs.append(((x * sides + y) * 2 + core, (px * sides + py) * 2 + pc))
    return lax.ppermute(value, "dp", pairs)


def along_first(sides, value, mask):
    return in_plane(sides, value, lambda x, y, c: (x, y ^ mask, c) if c == 0 else (x ^ mask, y, c))


def along_second(sides, value, mask):
    return in_plane(sides, value, lambda x, y, c: (x ^ mask, y, c) if c == 0 else (x, y ^ mask, c))


def swapped(sides, value):
    return in_plane(sides, value, lambda x, y, c: (x, y, 1 - c))


def gather_weights(mine, early, sides):
    sections = lax.axis_size("section")
    line = jnp.broadcast_to(mine, (sections, *mine.shape))
    line = lax.all_to_all(line, "section", 0, 0, tiled=True).reshape(2, -1, *mine.shape)
    came = [line] + [along_first(sides, line, mask) for mask in range(1, sides)]
    lines = [jnp.stack([got[part] for got in came]) for part in range(2)]
    wait = sum(nothing(value[0, : mine.shape[0]]) for value in early).astype(ROUND)
    lines = [block + wait for block in lines]
    with jax.named_scope("get_one"):
        one = [along_second(sides, lines[part], ORDERS[part][1]) for part in range(2)]
    pairs = paired(lines, one)
    with jax.named_scope("get_pair"):
        far = [along_second(sides, pairs[part], ORDERS[part][2]) for part in range(2)]
    with jax.named_scope("share"):
        early = [swapped(sides, block) for block in pairs]
        late = [swapped(sides, block) for block in far]
    return list(pairs) + far + early + late


def paired(kept, came):
    shape = kept[0].shape

    def kernel(*refs):
        for part in range(2):
            for k in range(2):
                refs[4 + part][k] = refs[2 * k + part][...]

    near = pl.BlockSpec(memory_space=pltpu.VMEM)
    return pl.pallas_call(
        kernel,
        out_shape=[jax.ShapeDtypeStruct((2, *shape), ROUND)] * 2,
        in_specs=[near] * 4,
        out_specs=[near] * 2,
        compiler_params=pltpu.CompilerParams(vmem_limit_bytes=SMALL << 20),
        name="paired",
    )(*kept, *came)


def nothing(value):
    return jnp.minimum(jnp.abs(value.astype(jnp.float32)), 0.0)


def wide(value):
    return value.astype(jnp.float32)


def added(blocks, which, swap, *came):
    first = which[0][0]

    def kernel(blocks, swap, *refs):
        for at, (turn, part) in enumerate(which):
            total = wide(blocks[1, turn, part]) + wide(swap[turn - first, part])
            if came:
                total = total + wide(refs[at][...])
            refs[len(came) + at][...] = total.astype(ROUND)

    near = pl.BlockSpec(memory_space=pltpu.VMEM)
    return pl.pallas_call(
        kernel,
        out_shape=[jax.ShapeDtypeStruct(blocks.shape[3:], ROUND)] * len(which),
        in_specs=[near] * (2 + len(came)),
        out_specs=[near] * len(which),
        compiler_params=pltpu.CompilerParams(vmem_limit_bytes=SMALL << 20),
        name="added",
    )(blocks, swap, *came)


def scatter_grads(blocks, sides):
    passed = blocks[0]
    with jax.named_scope("swap_far"):
        far = swapped(sides, passed[:2])
    with jax.named_scope("swap_near"):
        near = swapped(sides, passed[2:])
    two, three, one = [None] * 2, [None] * 2, [None] * 2
    two[0], two[1], three[0], three[1] = added(blocks, ((0, 0), (0, 1), (1, 0), (1, 1)), far)
    for part in range(2):
        with jax.named_scope("sum_two"):
            two[part] = along_second(sides, two[part], ORDERS[part][2])
    for part in range(2):
        with jax.named_scope("sum_three"):
            three[part] = along_second(sides, three[part], ORDERS[part][2])
    one = list(added(blocks, ((2, 0), (2, 1)), near, *two))
    for part in range(2):
        with jax.named_scope("sum_one"):
            one[part] = along_second(sides, one[part], ORDERS[part][1])
    lines = []
    for part in range(2):
        lines.append(wide(blocks[1, 3, part]) + wide(near[1, part]) + wide(three[part]) + wide(one[part]))
    line = jnp.concatenate(lines, axis=1)
    total = line[0]
    line = line.astype(ROUND)
    for mask in range(1, sides):
        total = total + wide(along_first(sides, line[mask], mask))
    tiles = lax.all_to_all(total.astype(ROUND), "section", 0, 0, tiled=True)
    return jnp.sum(wide(tiles), axis=0)


def on_device(stream, cotangent, weights, master, momentum):
    dp = lax.axis_size("dp")
    sides = int(round((dp // 2) ** 0.5))
    images = stream.shape[1] * dp
    share = weights.shape[1] // dp
    channels = weights.shape[2]
    z, at = lax.axis_index("section"), lax.axis_index("dp")
    place = jnp.stack([z, at // (2 * sides), at // 2 % sides, at % 2]).astype(jnp.int32)
    mine = lax.dynamic_slice_in_dim(weights[0], at * share, share, 0)
    pair = (2, stream.shape[2] * stream.shape[3], channels)
    first, last = (lax.dynamic_slice_in_dim(v, z, 1, 1).reshape(pair) for v in (stream, cotangent))
    gathered = gather_weights(mine, (first, last), sides)
    table = block_table(sides, *place[1:])
    blocks = image_grads(first, last, gathered, place, table, sides)
    blocks = blocks.reshape(2, sides, 2, sides, -1, share, channels)
    gradient = scatter_grads(blocks, sides) / images
    new_momentum = INERTIA * momentum[0] + gradient
    new_master = master[0] - STEP_SIZE * new_momentum
    chips = dp // 2
    copies = jnp.broadcast_to(new_master.astype(ROUND)[None], (chips, share, channels))
    same_core = [[2 * chip + core for chip in range(chips)] for core in range(2)]
    own = lax.all_to_all(copies, "dp", 0, 0, tiled=True, axis_index_groups=same_core)
    other = swapped(sides, own)
    even = (at % 2 == 0)
    both = [jnp.where(even, own, other), jnp.where(even, other, own)]
    new_weights = jnp.stack(both, axis=1).reshape(dp * share, channels)
    return (new_master[None], new_momentum[None], new_weights[None])


def solution(mesh):
    placed = (
        P(None, "dp", None, None, None),
        P(None, "dp", None, None, None),
        P("section", None, None),
        P("section", "dp", None),
        P("section", "dp", None),
    )
    return jax.shard_map(
        on_device,
        mesh=mesh,
        in_specs=placed,
        out_specs=(P("section", "dp", None), P("section", "dp", None), P("section", None, None)),
        check_vma=False,
    )
```

```python
import jax
import jax.numpy as jnp
from jax import lax
from jax.experimental import pallas as pl
from jax.experimental.pallas import tpu as pltpu
from jax.sharding import PartitionSpec as P

STEP_SIZE = 0.1
INERTIA = 0.9
ROUND = jnp.bfloat16
VMEM = 24
SMALL = 16


ORDERS = ((0, 1, 3, 2), (0, 3, 1, 2))


def rank_in(part, distance):
    if part == 0:
        return distance ^ (distance >> 1)
    return ((distance << 1) & 3) ^ (3 * (distance >> 1))


def block_table(sides, x, y, core):
    block = jnp.arange(2 * sides * sides)
    role = block % 2
    px, py = (block // (2 * sides)) ^ x, (block // 2 % sides) ^ y
    first, second = jnp.where(role == 0, py, px), jnp.where(role == 0, px, py)
    stays = (role == core).astype(jnp.int32)
    tables = []
    for part in range(2):
        turn = sides - 1 - rank_in(part, second)
        tables.append(((stays * sides + turn) * 2 + part) * sides + first)
    return jnp.concatenate(tables).astype(jnp.int32)


def in_strips(value, product):
    return jnp.concatenate([product(part) for part in jnp.split(value, 2)], axis=0)


def image_step(sides, sections, side, share, place, table, stream, cotangent, *refs):
    gathered, refs = refs[:8], refs[8:]
    out, refs = refs[0], refs[1:]
    x_in, d_in, w_all, saved_p, slopes, fwd_pad, bwd_pad, line_pad, x_sem, w_sem = refs
    z, x, y, core = place[0], place[1], place[2], place[3]
    channels = stream.shape[-1]
    pixels = side * side
    rows = w_all.shape[1]
    half = rows // 2
    slots = sections // 2
    blocks = 2 * sides * sides
    x_copy = pltpu.make_async_copy(stream, x_in, x_sem.at[0])
    d_copy = pltpu.make_async_copy(cotangent, d_in, x_sem.at[1])

    def lines(role, first, second):
        px = x ^ jnp.where(role == 0, second, first)
        py = y ^ jnp.where(role == 0, first, second)
        start = pl.multiple_of(((px * sides + py) * 2 + role) * share, 8)
        return pl.ds(start, share)

    copies = []
    for part in range(2):
        for which, role in ((0, core), (4, 1 - core)):
            early, late = gathered[which + part], gathered[which + 2 + part]
            sources = early.at[0], early.at[1], late.at[0], late.at[1]
            for i in range(sides):
                for j in range(sides):
                    where = lines(role, i, ORDERS[part][j])
                    target = w_all.at[pl.ds(part * slots, slots), where, :]
                    copies.append(pltpu.make_async_copy(sources[j].at[i], target, w_sem.at[len(copies)]))

    x_copy.start()
    for copy in copies:
        copy.start()
    d_copy.start()
    edge = jnp.zeros((side, 3 * channels), ROUND)
    for pad in (fwd_pad, bwd_pad):
        for k in range(2):
            pad[k, 0:side, :] = edge
            pad[k, side + pixels : 2 * side + pixels, :] = edge

    column = lax.broadcasted_iota(jnp.int32, (pixels, channels), 0) & (side - 1)
    not_first = column > 0
    not_last = column < side - 1

    def around(v):
        line_pad[8 : 8 + pixels, :] = v
        low = jnp.where(not_first, line_pad[7 : 7 + pixels, :], 0.0).astype(ROUND)
        high = jnp.where(not_last, line_pad[9 : 9 + pixels, :], 0.0).astype(ROUND)
        return low, high

    def band(pad, k, low, mid, high):
        body = pl.ds(side, pixels)
        pad[k, body, 0:channels] = low
        pad[k, body, channels : 2 * channels] = mid
        pad[k, body, 2 * channels : 3 * channels] = high

    def conv(pad, k, w):
        taps = jnp.concatenate([pad[k, a * side : a * side + pixels, :] for a in range(3)], axis=1)
        return in_strips(taps, lambda v: jnp.dot(v, w, preferred_element_type=jnp.float32))

    def activate(v, at):
        logistic = 1.0 / (1.0 + jnp.exp(-v))
        p = v * logistic
        slopes[at] = logistic + p * (1.0 - logistic)
        saved_p[at] = p.astype(ROUND)
        return p

    def forward(s, pair):
        x1, x2 = pair
        w = w_all.at[s]
        p = activate(x2, 2 * s)
        low, high = around(p)
        band(fwd_pad, 0, low, p.astype(ROUND), high)
        y1 = x1 + conv(fwd_pad, 0, w[0:half, :])
        p = activate(y1, 2 * s + 1)
        low, high = around(p)
        band(fwd_pad, 1, low, p.astype(ROUND), high)
        y2 = x2 + conv(fwd_pad, 1, w[half:rows, :])
        return y1, y2

    x_copy.wait()
    pair = x_in[0], x_in[1]
    for s in range(sections):
        if s % slots == 0:
            for copy in copies[s // slots * len(copies) // 2 : (s // slots + 1) * len(copies) // 2]:
                copy.wait()
        pair = forward(s, pair)

    def spread(k, e, w, s, base, at):
        low, high = around(e)
        band(bwd_pad, k, high, e.astype(ROUND), low)
        taps = jnp.concatenate(
            [bwd_pad[k, (2 - a) * side : (2 - a) * side + pixels, :] for a in range(3)], axis=1
        )
        across = jnp.concatenate(
            [w[base + tap * channels : base + (tap + 1) * channels, :] for tap in range(9)], axis=1
        )
        total = in_strips(
            taps,
            lambda v: lax.dot_general(v, across, (((1,), (1,)), ((), ())), preferred_element_type=jnp.float32),
        )
        wgrad = lax.dot_general(saved_p[at], taps, (((0,), (0,)), ((), ())), preferred_element_type=jnp.float32)
        for tap in range(9):
            row, end = base + tap * channels, base + (tap + 1) * channels
            while row < end:
                block = row // share
                stop = min(end, (block + 1) * share)
                n = table[s // slots * blocks + block] * slots + s % slots
                c = row - base - tap * channels
                piece = wgrad[c : c + stop - row, tap * channels : (tap + 1) * channels].astype(ROUND)
                out[n, row - block * share : stop - block * share, :] = piece
                row = stop
        return total * slopes[at]

    def backward(step, pair):
        d1, d2 = pair
        s = sections - 1 - step
        w = w_all.at[s]
        d1 = d1 + spread(0, d2, w, s, half, 2 * s + 1)
        d2 = d2 + spread(1, d1, w, s, 0, 2 * s)
        return d1, d2

    d_copy.wait()
    pair = d_in[0], d_in[1]
    for step in range(sections):
        pair = backward(step, pair)


def image_grads(stream, cotangent, gathered, place, table, sides):
    pixels, channels = stream.shape[1:]
    side = int(round(pixels**0.5))
    share = gathered[0].shape[3]
    sections = 2 * gathered[0].shape[2]
    rows = share * 2 * sides * sides
    far = pl.BlockSpec(memory_space=pl.ANY)
    kernel = lambda *refs: image_step(sides, sections, side, share, *refs)
    whole = 2 * sides * sides * sections
    return pl.pallas_call(
        kernel,
        out_shape=jax.ShapeDtypeStruct((whole, share, channels), ROUND),
        grid_spec=pltpu.PrefetchScalarGridSpec(
            num_scalar_prefetch=2,
            grid=(1,),
            in_specs=[far] * 10,
            out_specs=pl.BlockSpec(memory_space=pltpu.VMEM),
            scratch_shapes=[
                pltpu.VMEM((2, pixels, channels), jnp.float32),
                pltpu.VMEM((2, pixels, channels), jnp.float32),
                pltpu.VMEM((sections, rows, channels), ROUND),
                pltpu.VMEM((2 * sections, pixels, channels), ROUND),
                pltpu.VMEM((2 * sections, pixels, channels), jnp.float32),
                pltpu.VMEM((2, pixels + 2 * side, 3 * channels), ROUND),
                pltpu.VMEM((2, pixels + 2 * side, 3 * channels), ROUND),
                pltpu.VMEM((pixels + 16, channels), jnp.float32),
                pltpu.SemaphoreType.DMA((2,)),
                pltpu.SemaphoreType.DMA((4 * sides * sides,)),
            ],
        ),
        compiler_params=pltpu.CompilerParams(vmem_limit_bytes=VMEM << 20),
        name="image_step",
    )(place, table, stream, cotangent, *gathered)


def in_plane(sides, value, to):
    pairs = []
    for x in range(sides):
        for y in range(sides):
            for core in range(2):
                px, py, pc = to(x, y, core)
                pairs.append(((x * sides + y) * 2 + core, (px * sides + py) * 2 + pc))
    return lax.ppermute(value, "dp", pairs)


def along_first(sides, value, mask):
    return in_plane(sides, value, lambda x, y, c: (x, y ^ mask, c) if c == 0 else (x ^ mask, y, c))


def along_second(sides, value, mask):
    return in_plane(sides, value, lambda x, y, c: (x ^ mask, y, c) if c == 0 else (x, y ^ mask, c))


def swapped(sides, value):
    return in_plane(sides, value, lambda x, y, c: (x, y, 1 - c))


def gather_weights(mine, early, sides):
    sections = lax.axis_size("section")
    line = jnp.broadcast_to(mine, (sections, *mine.shape))
    line = lax.all_to_all(line, "section", 0, 0, tiled=True).reshape(2, -1, *mine.shape)
    came = [line] + [along_first(sides, line, mask) for mask in range(1, sides)]
    lines = [jnp.stack([got[part] for got in came]) for part in range(2)]
    wait = sum(nothing(value[0, : mine.shape[0]]) for value in early).astype(ROUND)
    lines = [block + wait for block in lines]
    with jax.named_scope("get_one"):
        one = [along_second(sides, lines[part], ORDERS[part][1]) for part in range(2)]
    pairs = paired(lines, one)
    with jax.named_scope("get_pair"):
        far = [along_second(sides, pairs[part], ORDERS[part][2]) for part in range(2)]
    with jax.named_scope("share"):
        early = [swapped(sides, block) for block in pairs]
        late = [swapped(sides, block) for block in far]
    return list(pairs) + far + early + late


def paired(kept, came):
    shape = kept[0].shape

    def kernel(*refs):
        for part in range(2):
            for k in range(2):
                refs[4 + part][k] = refs[2 * k + part][...]

    near = pl.BlockSpec(memory_space=pltpu.VMEM)
    return pl.pallas_call(
        kernel,
        out_shape=[jax.ShapeDtypeStruct((2, *shape), ROUND)] * 2,
        in_specs=[near] * 4,
        out_specs=[near] * 2,
        compiler_params=pltpu.CompilerParams(vmem_limit_bytes=SMALL << 20),
        name="paired",
    )(*kept, *came)


def nothing(value):
    return jnp.minimum(jnp.abs(value.astype(jnp.float32)), 0.0)


def wide(value):
    return value.astype(jnp.float32)


def added(blocks, which, swap, *came):
    first = which[0][0]

    def kernel(blocks, swap, *refs):
        for at, (turn, part) in enumerate(which):
            total = wide(blocks[1, turn, part]) + wide(swap[turn - first, part])
            if came:
                total = total + wide(refs[at][...])
            refs[len(came) + at][...] = total.astype(ROUND)

    near = pl.BlockSpec(memory_space=pltpu.VMEM)
    return pl.pallas_call(
        kernel,
        out_shape=[jax.ShapeDtypeStruct(blocks.shape[3:], ROUND)] * len(which),
        in_specs=[near] * (2 + len(came)),
        out_specs=[near] * len(which),
        compiler_params=pltpu.CompilerParams(vmem_limit_bytes=SMALL << 20),
        name="added",
    )(blocks, swap, *came)


def scatter_grads(blocks, sides):
    passed = blocks[0]
    with jax.named_scope("swap_far"):
        far = swapped(sides, passed[:2])
    with jax.named_scope("swap_near"):
        near = swapped(sides, passed[2:])
    two, three, one = [None] * 2, [None] * 2, [None] * 2
    two[0], two[1], three[0], three[1] = added(blocks, ((0, 0), (0, 1), (1, 0), (1, 1)), far)
    for part in range(2):
        with jax.named_scope("sum_two"):
            two[part] = along_second(sides, two[part], ORDERS[part][2])
    for part in range(2):
        with jax.named_scope("sum_three"):
            three[part] = along_second(sides, three[part], ORDERS[part][2])
    one = list(added(blocks, ((2, 0), (2, 1)), near, *two))
    for part in range(2):
        with jax.named_scope("sum_one"):
            one[part] = along_second(sides, one[part], ORDERS[part][1])
    lines = []
    for part in range(2):
        lines.append(wide(blocks[1, 3, part]) + wide(near[1, part]) + wide(three[part]) + wide(one[part]))
    line = jnp.concatenate(lines, axis=1)
    total = line[0]
    line = line.astype(ROUND)
    for mask in range(1, sides):
        total = total + wide(along_first(sides, line[mask], mask))
    tiles = lax.all_to_all(total.astype(ROUND), "section", 0, 0, tiled=True)
    return jnp.sum(wide(tiles), axis=0)


def on_device(stream, cotangent, weights, master, momentum):
    dp = lax.axis_size("dp")
    sides = int(round((dp // 2) ** 0.5))
    images = stream.shape[1] * dp
    share = weights.shape[1] // dp
    channels = weights.shape[2]
    z, at = lax.axis_index("section"), lax.axis_index("dp")
    place = jnp.stack([z, at // (2 * sides), at // 2 % sides, at % 2]).astype(jnp.int32)
    mine = lax.dynamic_slice_in_dim(weights[0], at * share, share, 0)
    pair = (2, stream.shape[2] * stream.shape[3], channels)
    first, last = (lax.dynamic_slice_in_dim(v, z, 1, 1).reshape(pair) for v in (stream, cotangent))
    gathered = gather_weights(mine, (first, last), sides)
    table = block_table(sides, *place[1:])
    blocks = image_grads(first, last, gathered, place, table, sides)
    blocks = blocks.reshape(2, sides, 2, sides, -1, share, channels)
    gradient = scatter_grads(blocks, sides) / images
    new_momentum = INERTIA * momentum[0] + gradient
    new_master = master[0] - STEP_SIZE * new_momentum
    chips = dp // 2
    copies = jnp.broadcast_to(new_master.astype(ROUND)[None], (chips, share, channels))
    same_core = [[2 * chip + core for chip in range(chips)] for core in range(2)]
    own = lax.all_to_all(copies, "dp", 0, 0, tiled=True, axis_index_groups=same_core)
    other = swapped(sides, own)
    even = (at % 2 == 0)
    gradient = gradient + nothing(own[0])
    new_momentum = INERTIA * momentum[0] + gradient
    new_master = master[0] - STEP_SIZE * new_momentum
    both = [jnp.where(even, own, other), jnp.where(even, other, own)]
    new_weights = jnp.stack(both, axis=1).reshape(dp * share, channels)
    return (new_master[None], new_momentum[None], new_weights[None])


def solution(mesh):
    placed = (
        P(None, "dp", None, None, None),
        P(None, "dp", None, None, None),
        P("section", None, None),
        P("section", "dp", None),
        P("section", "dp", None),
    )
    return jax.shard_map(
        on_device,
        mesh=mesh,
        in_specs=placed,
        out_specs=(P("section", "dp", None), P("section", "dp", None), P("section", None, None)),
        check_vma=False,
    )
```
